32 devices in a mesh: freq: 8 (over y, x, core), tile: 4 (over z).
Axes of the slice: x: 2, y: 2, z: 4, core: 2. Of those that a mesh axis runs over, the one named last changes fastest.
Arguments:
- left_factor: bfloat16 [128, 8, 32, 2, 16, 256], P('freq', 'tile'), may hold values from -1.5 to 1.5
- right_factor: bfloat16 [128, 8, 32, 2, 16, 256], P('freq', None, 'tile'), may hold values from -0.0625 to 0.0625
- tile_ranks: int32 [128, 8, 32], P('freq'), may hold values from 1 to 16
- tile_scales: float32 [128, 2, 8, 32], P('freq'), may hold values from 0.5 to 2
- recorded: float32 [128, 2, 8, 2048], P('freq', None, None, 'tile'), may hold values from -12 to 12
- step_sizes: float32 [128], P('freq'), may hold values from 0.2 to 0.6
- thresholds: float32 [8], replicated, may hold values from 0.1 to 0.5
Outputs:
- estimate: float32 [128, 2, 8, 8192], P('freq', None, None, 'tile')
The draws below stay inside these ranges and needn't reach their ends.
Inputs may be any that keep to these rules, and one draw needn't show every extreme that they name: `tile_ranks`: rank of each tile; rank slots at and above it carry no weight.
All inputs are finite; a program needn't handle non-finite values.
Results may differ from the reference program's by a relative error of at most 0.0058.
Values may be sent and summed in bfloat16 or wider, within the bound.
A program may use at most 128 MiB of HBM per device.

```python
import math
import jax
import jax.numpy as jnp
from jax import lax

TS = 256
R = 16
NV = 8
F = 128
NCT = 32
NRT = 8
NR = 2048
NC = 8192


def plant(entries, key, smallest, largest):
    longest = entries.shape.index(max(entries.shape))
    spots = []
    for shift in (0, 1):
        where = [jax.random.randint(jax.random.fold_in(key, axis), (), 0, length) for axis, length in enumerate(entries.shape)]
        where[longest] = (where[longest] + shift) % entries.shape[longest]
        spots.append(tuple(where))
    return entries.at[spots[0]].set(smallest).at[spots[1]].set(largest)


def steps_of(own_key, dims, split, low, largest):
    level = 1.0
    for axis_at, blocks in split:
        draws = jax.random.uniform(jax.random.fold_in(jax.random.fold_in(own_key, 6), axis_at), (blocks,), jnp.float32, low / len(split), largest / len(split))
        level = level * jnp.repeat(jnp.exp(draws), dims[axis_at] // blocks).reshape((-1,) + (1,) * (len(dims) - 1 - axis_at))
    return level


def normal_values(key, shape, deviation, bound, cuts=(), kind=jnp.bfloat16):
    result = deviation * jax.random.normal(key, shape, jnp.float32)
    if cuts:
        result = result * steps_of(key, shape, cuts, -0.22, 0.18)
    return jnp.clip(result, -bound, bound).astype(kind)


def setup_inputs(seed: int = 0) -> dict:
    keys = jax.random.split(jax.random.key(seed), 8)
    return {
        "left_factor": normal_values(keys[0], (F, NRT, NCT, 2, R, TS), R ** -0.5, 1.5, ((0, 8), (1, 4))),
        "right_factor": normal_values(keys[1], (F, NRT, NCT, 2, R, TS), NC ** -0.5, 0.0625, ((0, 8), (2, 4))),
        "tile_ranks": plant(jax.random.randint(keys[2], (F, NRT, NCT), 1, R + 1), jax.random.fold_in(keys[2], 1), 1, R).astype(jnp.int32),
        "tile_scales": jnp.clip(jnp.exp(math.log(2.0) - 1.3862944 * jax.random.uniform(keys[3], (F, 2, NRT, NCT), jnp.float32) ** steps_of(keys[3], (F, 2, NRT, NCT), ((0, 8),), -0.2, 0.2)), 0.5, 2.0),
        "recorded": normal_values(keys[4], (F, 2, NV, NR), 2.0, 12.0, ((0, 8), (3, 4)), jnp.float32),
        "step_sizes": jnp.clip(jnp.exp(math.log(0.6) - 1.0986123 * jax.random.uniform(keys[5], (F,), jnp.float32) ** steps_of(keys[5], (F,), ((0, 8),), -0.2, 0.2)), 0.2, 0.6),
        "thresholds": jnp.clip(jnp.exp(jax.random.uniform(keys[6], (NV,), jnp.float32, math.log(0.1), math.log(0.5))), 0.1, 0.5),
    }


def dft_tables(freq_index, time_count):
    times_row = jnp.arange(time_count, dtype=jnp.int32)
    phase_steps = (freq_index[:, None] * times_row[None, :] % time_count).astype(jnp.float32)
    angles = phase_steps * (2.0 * math.pi / time_count)
    scaling = jnp.where(freq_index == 0, math.sqrt(1.0 / time_count), math.sqrt(2.0 / time_count)).astype(jnp.float32)
    return (scaling[:, None] * jnp.cos(angles), scaling[:, None] * jnp.sin(angles))

def rounded(values):
    return lax.optimization_barrier(values.astype(jnp.bfloat16)).astype(jnp.float32)

def slot_weights(tile_ranks, tile_scales, rank_max):
    slot_index = jnp.arange(rank_max, dtype=jnp.int32)
    live_slots = (slot_index < tile_ranks[..., None]).astype(jnp.float32)
    return (tile_scales[:, 0] * tile_scales[:, 1])[..., None] * live_slots

def forward_one(left, right, weights, wavefield):
    tile_width = left.shape[-1]
    virtual = wavefield.shape[1]
    left_real = left[:, :, 0].astype(jnp.float32)
    left_imag = left[:, :, 1].astype(jnp.float32)
    right_real = right[:, :, 0].astype(jnp.float32)
    right_imag = right[:, :, 1].astype(jnp.float32)
    halves = rounded(wavefield).reshape(2, virtual, right.shape[1], tile_width)

    def project(matrix, vectors):
        return jnp.einsum('ijkp,vjp->ijkv', matrix, vectors)
    coef_real = project(right_real, halves[0]) + project(right_imag, halves[1])
    coef_imag = project(right_real, halves[1]) - project(right_imag, halves[0])
    coeffs = rounded(jnp.stack([coef_real, coef_imag], 2) * weights[:, :, None, :, None])

    def expand(matrix, vectors):
        return jnp.einsum('ijkq,ijkv->viq', matrix, vectors)
    image_real = expand(left_real, coeffs[:, :, 0]) - expand(left_imag, coeffs[:, :, 1])
    image_imag = expand(left_real, coeffs[:, :, 1]) + expand(left_imag, coeffs[:, :, 0])
    return jnp.stack([image_real, image_imag]).reshape(2, virtual, -1)

def adjoint_one(left, right, weights, residual):
    tile_width = left.shape[-1]
    virtual = residual.shape[1]
    left_real = left[:, :, 0].astype(jnp.float32)
    left_imag = left[:, :, 1].astype(jnp.float32)
    right_real = right[:, :, 0].astype(jnp.float32)
    right_imag = right[:, :, 1].astype(jnp.float32)
    halves = rounded(residual).reshape(2, virtual, left.shape[0], tile_width)

    def contract_left(matrix, vectors):
        return jnp.einsum('ijkq,viq->ijkv', matrix, vectors)
    dual_real = contract_left(left_real, halves[0]) + contract_left(left_imag, halves[1])
    dual_imag = contract_left(left_real, halves[1]) - contract_left(left_imag, halves[0])
    duals = rounded(jnp.stack([dual_real, dual_imag], 2) * weights[:, :, None, :, None])

    def spread(matrix, vectors):
        return jnp.einsum('ijkp,ijkv->vjp', matrix, vectors)
    grad_real = spread(right_real, duals[:, :, 0]) - spread(right_imag, duals[:, :, 1])
    grad_imag = spread(right_real, duals[:, :, 1]) + spread(right_imag, duals[:, :, 0])
    return jnp.stack([grad_real, grad_imag]).reshape(2, virtual, -1)

def reference(left_factor, right_factor, tile_ranks, tile_scales, recorded, step_sizes, thresholds):
    weights = slot_weights(tile_ranks, tile_scales, R)
    time_count = 2 * F
    cos_table, sin_table = dft_tables(jnp.arange(F, dtype=jnp.int32), time_count)
    highest = lax.Precision.HIGHEST

    def to_time(wavefield):
        return jnp.einsum('fvn,ft->nvt', wavefield[:, 0], cos_table, precision=highest) - jnp.einsum('fvn,ft->nvt', wavefield[:, 1], sin_table, precision=highest)

    def shrink(signal):
        excess = jnp.abs(signal) - thresholds[None, :, None]
        return jnp.sign(signal) * jnp.maximum(excess, 0.0)

    def to_freq(signal):
        real_part = jnp.einsum('nvt,ft->fvn', signal, cos_table, precision=highest)
        imag_part = -jnp.einsum('nvt,ft->fvn', signal, sin_table, precision=highest)
        return jnp.stack([real_part, imag_part], 1)

    def gradient(residual):
        return lax.map(lambda per_freq: adjoint_one(*per_freq), (left_factor, right_factor, weights, residual))

    def predict(wavefield):
        return lax.map(lambda per_freq: forward_one(*per_freq), (left_factor, right_factor, weights, wavefield))
    scaled = step_sizes[:, None, None, None]
    first = to_freq(shrink(to_time(scaled * gradient(recorded))))
    return to_freq(shrink(to_time(first + scaled * gradient(recorded - predict(first)))))
```

```python
import functools
import math

import jax
import jax.numpy as jnp
import numpy as np
from jax import lax
from jax.experimental import pallas as pl
from jax.experimental.pallas import tpu as pltpu
from jax.sharding import PartitionSpec as P

F = 128


def dft_tables(freq_index, time_count):
    times_row = jnp.arange(time_count, dtype=jnp.int32)
    phase_steps = (freq_index[:, None] * times_row[None, :] % time_count).astype(jnp.float32)
    angles = phase_steps * (2.0 * math.pi / time_count)
    scaling = jnp.where(
        freq_index == 0, math.sqrt(1.0 / time_count), math.sqrt(2.0 / time_count)
    ).astype(jnp.float32)
    return (scaling[:, None] * jnp.cos(angles), scaling[:, None] * jnp.sin(angles))


def slot_weights(tile_ranks, tile_scales, rank_max):
    slot_index = jnp.arange(rank_max, dtype=jnp.int32)
    live_slots = (slot_index < tile_ranks[..., None]).astype(jnp.float32)
    return (tile_scales[:, 0] * tile_scales[:, 1])[..., None] * live_slots


def per_device_plain(
    left_factor, right_factor, tile_ranks, tile_scales, recorded, step_sizes, thresholds
):
    freqs_here = left_factor.shape[0]
    rows_here = left_factor.shape[1]
    col_tiles = left_factor.shape[2]
    rank_max = left_factor.shape[4]
    tile_width = left_factor.shape[5]
    row_tiles = right_factor.shape[1]
    cols_here = right_factor.shape[2]
    virtual = recorded.shape[2]
    tile_pos = lax.axis_index("tile")
    columns_here = cols_here * tile_width
    time_count = 2 * F
    highest = lax.Precision.HIGHEST
    weights = slot_weights(tile_ranks, tile_scales, rank_max)
    weights_right = lax.dynamic_slice_in_dim(weights, tile_pos * cols_here, cols_here, 2)
    weights_left = lax.dynamic_slice_in_dim(weights, tile_pos * rows_here, rows_here, 1)
    left_real = left_factor[:, :, :, 0]
    left_imag = left_factor[:, :, :, 1]
    right_real = right_factor[:, :, :, 0]
    right_imag = right_factor[:, :, :, 1]
    cos_all, sin_all = dft_tables(jnp.arange(F, dtype=jnp.int32), time_count)

    def gradient(residual):
        halves = residual.astype(jnp.bfloat16).reshape(
            freqs_here, 2, virtual, rows_here, tile_width
        )

        def contract_left(matrix, vectors):
            return jnp.einsum(
                "fijkq,fviq->fijkv", matrix, vectors, preferred_element_type=jnp.float32
            )

        dual_real = contract_left(left_real, halves[:, 0]) + contract_left(left_imag, halves[:, 1])
        dual_imag = contract_left(left_real, halves[:, 1]) - contract_left(left_imag, halves[:, 0])
        duals = (
            jnp.stack([dual_real, dual_imag], 3) * weights_left[:, :, :, None, :, None]
        ).astype(jnp.bfloat16)
        duals = duals.reshape(freqs_here, rows_here, col_tiles, 2, rank_max * virtual)
        arrived = lax.all_to_all(duals, "tile", split_axis=2, concat_axis=1, tiled=True)
        arrived = arrived.reshape(freqs_here, row_tiles, cols_here, 2, rank_max, virtual)

        def spread(matrix, vectors):
            return jnp.einsum(
                "fijkp,fijkv->fvjp", matrix, vectors, preferred_element_type=jnp.float32
            )

        grad_real = spread(right_real, arrived[:, :, :, 0]) - spread(
            right_imag, arrived[:, :, :, 1]
        )
        grad_imag = spread(right_real, arrived[:, :, :, 1]) + spread(
            right_imag, arrived[:, :, :, 0]
        )
        return jnp.stack([grad_real, grad_imag], 1).reshape(freqs_here, 2, virtual, columns_here)

    def to_time(wavefield):
        swapped = lax.all_to_all(wavefield, "freq", split_axis=3, concat_axis=0, tiled=True)
        return jnp.einsum("fvn,ft->nvt", swapped[:, 0], cos_all, precision=highest) - jnp.einsum(
            "fvn,ft->nvt", swapped[:, 1], sin_all, precision=highest
        )

    def shrink(signal):
        excess = jnp.abs(signal) - thresholds[None, :, None]
        return jnp.sign(signal) * jnp.maximum(excess, 0.0)

    def to_freq(signal):
        real_part = jnp.einsum("nvt,ft->fvn", signal, cos_all, precision=highest)
        imag_part = -jnp.einsum("nvt,ft->fvn", signal, sin_all, precision=highest)
        return lax.all_to_all(
            jnp.stack([real_part, imag_part], 1), "freq", split_axis=0, concat_axis=3, tiled=True
        )

    scaled = step_sizes[:, None, None, None]
    first = to_freq(shrink(to_time(scaled * gradient(recorded))))
    halves = first.astype(jnp.bfloat16).reshape(freqs_here, 2, virtual, cols_here, tile_width)

    def project(matrix, vectors):
        return jnp.einsum("fijkp,fvjp->fijkv", matrix, vectors, preferred_element_type=jnp.float32)

    coef_real = project(right_real, halves[:, 0]) + project(right_imag, halves[:, 1])
    coef_imag = project(right_real, halves[:, 1]) - project(right_imag, halves[:, 0])
    coeffs = (jnp.stack([coef_real, coef_imag], 3) * weights_right[:, :, :, None, :, None]).astype(
        jnp.bfloat16
    )
    coeffs = coeffs.reshape(freqs_here, row_tiles, cols_here, 2, rank_max * virtual)
    arrived = lax.all_to_all(coeffs, "tile", split_axis=1, concat_axis=2, tiled=True)
    arrived = arrived.reshape(freqs_here, rows_here, col_tiles, 2, rank_max, virtual)

    def expand(matrix, vectors):
        return jnp.einsum("fijkq,fijkv->fviq", matrix, vectors, preferred_element_type=jnp.float32)

    image_real = expand(left_real, arrived[:, :, :, 0]) - expand(left_imag, arrived[:, :, :, 1])
    image_imag = expand(left_real, arrived[:, :, :, 1]) + expand(left_imag, arrived[:, :, :, 0])
    return to_freq(
        shrink(
            to_time(
                first
                + scaled
                * gradient(
                    recorded
                    - jnp.stack([image_real, image_imag], 1).reshape(
                        freqs_here, 2, virtual, rows_here * tile_width
                    )
                )
            )
        )
    )


LANES = 128


def lane_ids(rows, lanes):
    return lax.broadcasted_iota(jnp.int32, (rows, lanes), 1)


def nt_dot(a, b):
    return lax.dot_general(a, b, (((1,), (1,)), ((), ())), preferred_element_type=jnp.float32)


def nn_dot(a, b):
    return jnp.dot(a, b, preferred_element_type=jnp.float32)


def swap(values):
    return pltpu.roll(values, LANES // 2, 1)


def part_sign(rows):
    return jnp.where(lane_ids(rows, LANES) < LANES // 2, 1.0, -1.0)


def split_two(values):
    high = values.astype(jnp.bfloat16)
    return high, (values - high.astype(jnp.float32)).astype(jnp.bfloat16)


def stacked_parts(ranks, scales):
    high = scales.astype(jnp.bfloat16)
    rest = scales - high.astype(jnp.float32)
    middle = rest.astype(jnp.bfloat16)
    low = (rest - middle.astype(jnp.float32)).astype(jnp.bfloat16)
    return high, middle, low, ranks.astype(jnp.float32).astype(jnp.bfloat16)


def weights_of(product, rows, rank):
    high, middle, low, ranks = [product[n * rows : (n + 1) * rows] for n in range(4)]
    slot = (lane_ids(rows, product.shape[1]) % rank).astype(jnp.float32)
    return jnp.where(slot < ranks - 0.5, high + middle + low, 0.0)


class Exchange:
    def __init__(self, axis, send, recv, send_sem, recv_sem):
        self.axis, self.send, self.recv = axis, send, recv
        self.send_sem, self.recv_sem = send_sem, recv_sem
        self.size = send.shape[2]
        self.me = lax.axis_index(axis)

    def peers(self):
        return [lax.rem(self.me + step, self.size) for step in range(1, self.size)]

    def start(self, half, block):
        for peer in self.peers():
            pltpu.make_async_remote_copy(
                src_ref=self.send.at[half, block, peer],
                dst_ref=self.recv.at[half, block, self.me],
                send_sem=self.send_sem,
                recv_sem=self.recv_sem.at[half, block],
                device_id={self.axis: peer},
                device_id_type=pl.DeviceIdType.MESH,
            ).start()
        self.recv[half, block, self.me] = self.send[half, block, self.me]

    def wait(self, half, block):
        others = pl.ds(0, self.size - 1)
        pltpu.make_async_remote_copy(
            src_ref=self.send.at[half, block, others],
            dst_ref=self.recv.at[half, block, others],
            send_sem=self.send_sem,
            recv_sem=self.recv_sem.at[half, block],
            device_id={self.axis: self.peers()[0]},
            device_id_type=pl.DeviceIdType.MESH,
        ).wait_recv()

    def finish(self):
        others = pl.ds(0, self.size - 1)
        pltpu.make_async_remote_copy(
            src_ref=self.send.at[:, :, others],
            dst_ref=self.recv.at[:, :, others],
            send_sem=self.send_sem,
            recv_sem=self.recv_sem.at[0, 0],
            device_id={self.axis: self.peers()[0]},
            device_id_type=pl.DeviceIdType.MESH,
        ).wait_send()


def whole_kernel(
    levels_ref, steps_ref, tables_hbm, left_hbm, right_hbm, recorded_hbm, ranks_hbm, scales_hbm,
    out_hbm,
    tables, left, right, recorded, ranks_ref, scales_ref, out_ref,
    left_sem, right_sem, small_sem, out_sem,
    weight_left, weight_right, residual, narrow, gathered, fields, kept,
    tile_send, tile_recv, freq_send, freq_recv, tile_ssem, tile_rsem, freq_ssem, freq_rsem,
):
    freqs, rows, tile_size, _, _, rank, width = left.shape
    row_tiles = right.shape[1]
    virtual = recorded.shape[2]
    per_half = LANES // (2 * rank)
    lanes_each = width // LANES
    halves, blocks = tile_send.shape[1:3]
    at_once = tile_send.shape[4]
    wide_blocks = freq_send.shape[2]
    wide_once = freqs // wide_blocks
    per_wide = wide_once // at_once
    both = 2 * virtual
    pieces = halves * blocks
    share = tile_size * LANES
    first_row = lax.axis_index("tile") * rows
    sign = part_sign(virtual)
    over_tile = [
        Exchange("tile", tile_send.at[n], tile_recv.at[n], tile_ssem.at[n], tile_rsem.at[n])
        for n in range(tile_send.shape[0])
    ]
    over_freq = [
        Exchange("freq", freq_send.at[n], freq_recv.at[n], freq_ssem.at[n], freq_rsem.at[n])
        for n in range(freq_send.shape[0])
    ]
    small = [
        pltpu.make_async_copy(source, target, small_sem.at[n])
        for n, (source, target) in enumerate(
            [(ranks_hbm, ranks_ref), (scales_hbm, scales_ref), (recorded_hbm, recorded),
             (tables_hbm, tables)]
        )
    ]

    def place(piece):
        return piece // blocks, piece % blocks

    def fetch_left(piece):
        half, block = place(piece)
        part = (pl.ds(block * at_once, at_once), slice(None), slice(None), pl.ds(half * per_half, per_half))
        return pltpu.make_async_copy(left_hbm.at[part], left.at[part], left_sem.at[half, block])

    def fetch_right(piece):
        half, block = place(piece)
        part = (pl.ds(block * at_once, at_once), slice(None), pl.ds(half * per_half, per_half))
        return pltpu.make_async_copy(right_hbm.at[part], right.at[part], right_sem.at[half, block])

    def each_freq(block, body):
        for inner in range(at_once):
            body(inner, block * at_once + inner)

    def left_rows(freq, row, half):
        own = pl.ds(half * per_half, per_half)
        return jnp.concatenate(
            [
                left[freq, row, tile, own, part].reshape(per_half * rank, width)
                for tile in range(tile_size)
                for part in range(2)
            ],
            0,
        )

    def dual(exchange, half, block, inner, freq, field_of):
        duals = []
        for row in range(rows):
            product = nt_dot(field_of(row), left_rows(freq, row, half))
            weight = weight_left[half, pl.ds(freq * row_tiles + first_row + row, 1), :]
            duals.append(
                [
                    (
                        product[:virtual, at : at + LANES] * sign
                        + swap(product[virtual:, at : at + LANES])
                    )
                    * weight[:, at : at + LANES]
                    for at in range(0, share, LANES)
                ]
            )
        for tile in range(tile_size):
            exchange.send[half, block, tile, inner] = jnp.concatenate(
                [duals[row][tile] for row in range(rows)], 0
            ).astype(jnp.bfloat16)

    def first_dual(piece):
        half, block = place(piece)

        def body(inner, freq):
            dual(
                over_tile[0], half, block, inner, freq,
                lambda row: recorded[freq, :, :, row * width : (row + 1) * width]
                .reshape(both, width)
                .astype(jnp.bfloat16),
            )

        each_freq(block, body)
        over_tile[0].start(half, block)

    owner = lane_ids(both, LANES) % (LANES // 2) // rank
    owns = [jnp.where(owner == n, 1.0, 0.0).astype(jnp.bfloat16) for n in range(per_half)]

    def spread(tiles, target, piece):
        half, block = place(piece)
        tiles.wait(half, block)
        own = pl.ds(half * per_half, per_half)

        def body(inner, freq):
            forms = []
            for tile in range(tile_size):
                arrived = tiles.recv[half, block, tile, inner].astype(jnp.float32)
                for row in range(rows):
                    part = arrived[row * virtual : (row + 1) * virtual]
                    forms.append(
                        jnp.concatenate([part * sign, swap(part)], 0).astype(jnp.bfloat16)
                    )
            matrix = jnp.concatenate(
                [jnp.concatenate([form * own_n for form in forms], 1) for own_n in owns], 0
            )
            factors = jnp.concatenate(
                [
                    right[freq, row, own, part].reshape(per_half * rank, width)
                    for row in range(row_tiles)
                    for part in range(2)
                ],
                0,
            )
            total = nn_dot(matrix, factors) * steps_ref[freq]
            within = (block % per_wide) * at_once + inner
            for col in range(per_half):
                for lane in range(lanes_each):
                    narrow[col * lanes_each + lane, pl.ds(within * both, both), :] = total[
                        col * both : (col + 1) * both, lane * LANES : (lane + 1) * LANES
                    ]

        each_freq(block, body)

        @pl.when(block % per_wide == per_wide - 1)
        def _():
            to = block // per_wide

            @pl.loop(0, per_half * lanes_each)
            def _(peer):
                for source in range(virtual):
                    target.send[half, to, peer, source] = narrow[
                        peer, pl.ds(source, 2 * wide_once, stride=virtual), :
                    ].astype(jnp.bfloat16)

            target.start(half, to)

    def shrink(second, source, target, half):
        for block in range(wide_blocks):
            source.wait(half, block)
        times = tables.shape[1]
        turn = jnp.where(
            lax.broadcasted_iota(jnp.int32, (times, 2 * LANES), 0) % 2 == 0, 1.0, -1.0
        )
        lane = lane_ids(1, 2 * LANES)
        for pair in range(virtual // 2):
            spectrum = jnp.concatenate(
                [
                    jnp.concatenate(
                        [
                            source.recv[half, block, peer, 2 * pair + n]
                            for peer in range(source.size)
                            for block in range(wide_blocks)
                        ],
                        0,
                    )
                    for n in range(2)
                ],
                1,
            )
            signal = nn_dot(tables[0], spectrum) + nn_dot(tables[1], spectrum)
            if second:
                signal += kept[half, pair]
            level = jnp.where(lane < LANES, levels_ref[2 * pair], levels_ref[2 * pair + 1])
            shrunk = signal - jnp.minimum(jnp.maximum(signal, -level), level)
            if not second:
                mean = jnp.sum(shrunk * turn, 0, keepdims=True) * (1.0 / times)
                kept[half, pair] = shrunk - turn * mean
            high, low = split_two(shrunk)
            back = (
                nn_dot(tables[2], high) + nn_dot(tables[3], high) + nn_dot(tables[2], low)
            ).astype(jnp.bfloat16)
            tall = 2 * wide_once
            for peer in range(target.size):
                for block in range(wide_blocks):
                    at = (peer * wide_blocks + block) * tall
                    for n in range(2):
                        target.send[half, block, peer, 2 * pair + n] = back[
                            at : at + tall, n * LANES : (n + 1) * LANES
                        ]
        for block in range(wide_blocks):
            target.start(half, block)

    def unshuffle(source, half, block, store):
        source.wait(half, block)
        tall = 2 * wide_once

        @pl.loop(0, source.size)
        def _(peer):
            for n in range(virtual):
                gathered[peer, n * tall : (n + 1) * tall] = source.recv[
                    half, block, peer, n
                ].astype(jnp.float32)

        @pl.loop(0, wide_once)
        def _(freq):
            for peer in range(source.size):
                store(
                    freq,
                    peer,
                    jnp.concatenate(
                        [
                            gathered[peer, pl.ds(2 * freq + part, virtual, stride=tall), :]
                            for part in range(2)
                        ],
                        0,
                    ).astype(jnp.bfloat16),
                )

    def store_field(freq, peer, values):
        fields[freq, :, peer * LANES : (peer + 1) * LANES] = values

    low_part = lane_ids(virtual, LANES) % (LANES // 2) < rows * rank

    def project(target, half, block):
        groups = row_tiles // per_half
        per_group = per_half // rows

        def body(inner, freq):
            within = (block % per_wide) * at_once + inner
            coefs = []
            for col in range(per_half):
                field = fields[within, :, col * width : (col + 1) * width]
                factors = jnp.concatenate(
                    [
                        right[
                            freq, group * per_half : (group + 1) * per_half,
                            half * per_half + col, part,
                        ].reshape(per_half * rank, width)
                        for group in range(groups)
                        for part in range(2)
                    ],
                    0,
                )
                product = nt_dot(field, factors)
                weight = weight_right[freq, pl.ds(half * per_half + col, 1), :]
                coefs.append(
                    [
                        (
                            product[:virtual, at : at + LANES] * sign
                            + swap(product[virtual:, at : at + LANES])
                        )
                        * weight[:, at : at + LANES]
                        for at in range(0, groups * LANES, LANES)
                    ]
                )
            shift = rows * rank
            for group in range(groups):
                lower, upper = [], []
                for col in range(0, per_half, per_group):
                    a, b = coefs[col][group], coefs[col + 1][group]
                    lower.append(jnp.where(low_part, a, pltpu.roll(b, shift, 1)))
                    upper.append(jnp.where(low_part, pltpu.roll(a, LANES - shift, 1), b))
                for n, packed in enumerate((lower, upper)):
                    target.send[half, block, group * per_group + n, inner] = jnp.concatenate(
                        packed, 0
                    ).astype(jnp.bfloat16)

        each_freq(block, body)
        target.start(half, block)

    row_owner = lane_ids(both, LANES) % (rows * rank) // rank
    row_owns = [jnp.where(row_owner == n, 1.0, 0.0).astype(jnp.bfloat16) for n in range(rows)]

    def image(source, half, block, inner, freq):
        per_group = per_half // rows
        forms = []
        for tile in range(tile_size):
            arrived = source.recv[half, block, tile, inner].astype(jnp.float32)
            for n in range(rows):
                part = arrived[n * virtual : (n + 1) * virtual]
                forms.append(jnp.concatenate([part * sign, swap(part)], 0).astype(jnp.bfloat16))
        matrix = jnp.concatenate(
            [jnp.concatenate([form * own for form in forms], 1) for own in row_owns], 0
        )
        factors = jnp.concatenate(
            [
                left[freq, row, tile, half * per_half + n * per_group + col, part]
                for tile in range(tile_size)
                for n in range(rows)
                for part in range(2)
                for col in range(per_group)
                for row in range(rows)
            ],
            0,
        )
        return nn_dot(matrix, factors)

    def first_image(block):
        over_tile[1].wait(0, block)

        def body(inner, freq):
            part = image(over_tile[1], 0, block, inner, freq)
            for row in range(rows):
                residual[freq, row] = (
                    recorded[freq, :, :, row * width : (row + 1) * width].reshape(both, width)
                    - part[row * both : (row + 1) * both]
                )

        each_freq(block, body)

    def last_image(block):
        over_tile[1].wait(1, block)

        def body(inner, freq):
            part = image(over_tile[1], 1, block, inner, freq)
            for row in range(rows):
                residual[freq, row] = residual[freq, row] - part[row * both : (row + 1) * both]
            dual(
                over_tile[2], 0, block, inner, freq,
                lambda row: residual[freq, row].astype(jnp.bfloat16),
            )

        each_freq(block, body)
        over_tile[2].start(0, block)

    def last_dual(block):
        def body(inner, freq):
            dual(
                over_tile[2], 1, block, inner, freq,
                lambda row: residual[freq, row].astype(jnp.bfloat16),
            )

        each_freq(block, body)
        over_tile[2].start(1, block)

    for copy in small[:2]:
        copy.start()
    for piece in range(AHEAD):
        fetch_left(piece).start()
        if piece == 0:
            small[2].start()

    barrier = pltpu.get_barrier_semaphore()
    count = 0
    for exchange in (over_tile[0], over_freq[0]):
        for peer in exchange.peers():
            pl.semaphore_signal(
                barrier, inc=1, device_id={exchange.axis: peer},
                device_id_type=pl.DeviceIdType.MESH,
            )
            count += 1

    for copy in small[:2]:
        copy.wait()
    tiles = ranks_ref.shape[2]
    lines = freqs * row_tiles
    parts = stacked_parts(
        ranks_ref[...].reshape(lines, tiles),
        (scales_ref[:, 0] * scales_ref[:, 1]).reshape(lines, tiles),
    )
    stacked = jnp.concatenate(parts, 0)
    for half in range(halves):
        lane = lane_ids(tiles, share)
        owner_tile = (
            lane // LANES * (halves * per_half) + half * per_half + lane % (LANES // 2) // rank
        )
        pick = jnp.where(
            owner_tile == lax.broadcasted_iota(jnp.int32, (tiles, share), 0), 1.0, 0.0
        ).astype(jnp.bfloat16)
        weight_left[half] = weights_of(nn_dot(stacked, pick), lines, rank)

    small[2].wait()
    pl.semaphore_wait(barrier, count)

    @pl.loop(0, pieces + TILE_LAG)
    def _(step):
        @pl.when(step + AHEAD < pieces)
        def _():
            fetch_left(step + AHEAD).start()

        @pl.when(step < pieces)
        def _():
            fetch_right(step).start()
            fetch_left(step).wait()
            first_dual(step)

        @pl.when(step == pieces - 1)
        def _():
            small[3].start()
            cols = weight_right.shape[1]
            mine = lax.axis_index("tile") * cols
            select = jnp.where(
                lane_ids(cols, tiles) == mine + lax.broadcasted_iota(jnp.int32, (cols, tiles), 0),
                1.0, 0.0,
            ).astype(jnp.bfloat16)
            turned = jnp.concatenate([nt_dot(select, part) for part in parts], 0).astype(
                jnp.bfloat16
            )
            lanes = weight_right.shape[2]
            lane = lane_ids(lines, lanes)
            owner_row = lane // LANES * per_half + lane % (LANES // 2) // rank

            @pl.loop(0, freqs)
            def _(freq):
                pick = jnp.where(
                    lax.broadcasted_iota(jnp.int32, (lines, lanes), 0)
                    == owner_row + freq * row_tiles,
                    1.0, 0.0,
                ).astype(jnp.bfloat16)
                weight_right[freq] = weights_of(nn_dot(turned, pick), cols, rank)

            small[3].wait()

        @pl.when(step == FIRST_SHRINK)
        def _():
            shrink(False, over_freq[0], over_freq[1], 0)

        @pl.when(step >= TILE_LAG)
        def _():
            piece = step - TILE_LAG
            fetch_right(piece).wait()
            spread(over_tile[0], over_freq[0], piece)

    def second_half(half, block):
        unshuffle(over_freq[1], half, block, store_field)

        @pl.loop(0, per_wide)
        def _(n):
            project(over_tile[1], half, block * per_wide + n)

    @pl.loop(0, wide_blocks)
    def _(block):
        second_half(0, block)

    shrink(False, over_freq[0], over_freq[1], 1)

    @pl.loop(0, wide_blocks)
    def _(block):
        second_half(1, block)

        @pl.loop(0, per_wide)
        def _(n):
            first_image(block * per_wide + n)

    @pl.loop(0, blocks)
    def _(block):
        last_image(block)

    @pl.loop(0, pieces)
    def _(step):
        @pl.when(step < blocks)
        def _():
            last_dual(step)

        @pl.when(step == SECOND_SHRINK)
        def _():
            shrink(True, over_freq[2], over_freq[3], 0)

        spread(over_tile[2], over_freq[2], step)

    shrink(True, over_freq[2], over_freq[3], 1)

    half_width = per_half * width

    def put(half, block):
        part = (
            pl.ds(block * wide_once, wide_once), slice(None), pl.ds(half * half_width, half_width)
        )
        return pltpu.make_async_copy(out_ref.at[half, block], out_hbm.at[part], out_sem.at[half, block])

    for half in range(halves):
        @pl.loop(0, wide_blocks)
        def _(block):
            def store(freq, peer, values):
                out_ref[half, block, freq, :, peer * LANES : (peer + 1) * LANES] = values

            unshuffle(over_freq[3], half, block, store)
            put(half, block).start()

    for half in range(halves):
        for block in range(wide_blocks):
            put(half, block).wait()
    for exchange in over_tile + over_freq:
        exchange.finish()


AHEAD = 3
TILE_LAG = 3
FIRST_SHRINK = 9
SECOND_SHRINK = 6


def table_parts():
    times = 2 * F
    freq = np.arange(F)[:, None]
    angles = (freq * np.arange(times)[None, :] % times) * (2.0 * math.pi / times)
    scaling = np.where(freq == 0, math.sqrt(1.0 / times), math.sqrt(2.0 / times))
    table = np.stack([scaling * np.cos(angles), -scaling * np.sin(angles)], 1)
    table = table.reshape(2 * F, times).astype(np.float32)
    high = table.astype(jnp.bfloat16)
    low = (table - high.astype(np.float32)).astype(jnp.bfloat16)
    return jnp.asarray(np.stack([high.T, low.T, high, low]))


def vmem():
    return pl.BlockSpec(memory_space=pltpu.VMEM)


def smem():
    return pl.BlockSpec(memory_space=pltpu.SMEM)


def per_device(
    left_factor, right_factor, tile_ranks, tile_scales, recorded, step_sizes, thresholds
):
    freqs, rows_here, col_tiles, _, rank, width = left_factor.shape
    row_tiles, cols_here = right_factor.shape[1:3]
    virtual = recorded.shape[2]
    tile_size = col_tiles // cols_here
    freq_size = lax.axis_size("freq")
    per_half = LANES // (2 * rank)
    halves = cols_here // per_half
    wide_once = 8
    wide_blocks = freqs // wide_once
    at_once = 4
    blocks = freqs // at_once
    both = 2 * virtual
    left_factor = left_factor.reshape(freqs, rows_here, tile_size, cols_here, 2, rank, width)
    out_shape = (freqs, both, cols_here * width)
    dma = pltpu.SemaphoreType.DMA
    tables = table_parts()
    bf16, f32 = jnp.bfloat16, jnp.float32
    tile_buffer = pltpu.VMEM(
        (3, halves, blocks, tile_size, at_once, rows_here * virtual, LANES), bf16
    )
    freq_buffer = pltpu.VMEM(
        (4, halves, wide_blocks, freq_size, virtual, 2 * wide_once, LANES), bf16
    )
    estimate = pl.pallas_call(
        whole_kernel,
        out_shape=jax.ShapeDtypeStruct(out_shape, bf16),
        in_specs=[smem(), smem()] + [pl.BlockSpec(memory_space=pl.ANY)] * 6,
        out_specs=pl.BlockSpec(memory_space=pl.ANY),
        scratch_shapes=[
            pltpu.VMEM(tables.shape, bf16),
            pltpu.VMEM(left_factor.shape, bf16),
            pltpu.VMEM(right_factor.shape, bf16),
            pltpu.VMEM(recorded.shape, f32),
            pltpu.VMEM(tile_ranks.shape, jnp.int32),
            pltpu.VMEM(tile_scales.shape, f32),
            pltpu.VMEM((halves, wide_blocks, wide_once, both, per_half * width), bf16),
            dma((halves, blocks)),
            dma((halves, blocks)),
            dma((4,)),
            dma((halves, wide_blocks)),
            pltpu.VMEM((halves, freqs * row_tiles, tile_size * LANES), f32),
            pltpu.VMEM((freqs, cols_here, row_tiles * 2 * rank), f32),
            pltpu.VMEM((freqs, rows_here, both, width), f32),
            pltpu.VMEM((freq_size, wide_once * both, LANES), f32),
            pltpu.VMEM((freq_size, wide_once * both, LANES), f32),
            pltpu.VMEM((wide_once, both, per_half * width), bf16),
            pltpu.VMEM((halves, virtual // 2, 2 * F, 2 * LANES), f32),
            tile_buffer,
            tile_buffer,
            freq_buffer,
            freq_buffer,
            dma((3,)),
            dma((3, halves, blocks)),
            dma((4,)),
            dma((4, halves, wide_blocks)),
        ],
        compiler_params=pltpu.CompilerParams(
            vmem_limit_bytes=58 << 20,
            collective_id=0,
            has_side_effects=True,
        ),
    )(
        thresholds, step_sizes, tables, left_factor, right_factor, recorded, tile_ranks,
        tile_scales,
    )
    return estimate.astype(jnp.float32).reshape(freqs, 2, virtual, cols_here * width)


def either(*arrays):
    left_factor, right_factor = arrays[:2]
    freqs, rows_here, col_tiles = left_factor.shape[:3]
    row_tiles, cols_here = right_factor.shape[1:3]
    rank, width = left_factor.shape[4:]
    freq_size = lax.axis_size("freq")
    aligned = (
        rank == 16
        and rows_here == 2
        and width % LANES == 0
        and cols_here == 2 * (LANES // (2 * rank))
        and freq_size == LANES // (2 * rank) * (width // LANES)
        and row_tiles % (LANES // (2 * rank)) == 0
        and row_tiles == rows_here * lax.axis_size("tile")
        and col_tiles == cols_here * lax.axis_size("tile")
        and arrays[4].shape[2] == 8
        and freqs % 8 == 0
        and freqs * freq_size == F
    )
    return (per_device if aligned else per_device_plain)(*arrays)


def solution(mesh):
    return jax.shard_map(
        either,
        mesh=mesh,
        in_specs=(
            P("freq", "tile", None, None, None, None),
            P("freq", None, "tile", None, None, None),
            P("freq", None, None),
            P("freq", None, None, None),
            P("freq", None, None, "tile"),
            P("freq"),
            P(),
        ),
        out_specs=P("freq", None, None, "tile"),
        check_vma=False,
    )
```

```python
import functools
import math

import jax
import jax.numpy as jnp
import numpy as np
from jax import lax
from jax.experimental import pallas as pl
from jax.experimental.pallas import tpu as pltpu
from jax.sharding import PartitionSpec as P

F = 128


def dft_tables(freq_index, time_count):
    times_row = jnp.arange(time_count, dtype=jnp.int32)
    phase_steps = (freq_index[:, None] * times_row[None, :] % time_count).astype(jnp.float32)
    angles = phase_steps * (2.0 * math.pi / time_count)
    scaling = jnp.where(
        freq_index == 0, math.sqrt(1.0 / time_count), math.sqrt(2.0 / time_count)
    ).astype(jnp.float32)
    return (scaling[:, None] * jnp.cos(angles), scaling[:, None] * jnp.sin(angles))


def slot_weights(tile_ranks, tile_scales, rank_max):
    slot_index = jnp.arange(rank_max, dtype=jnp.int32)
    live_slots = (slot_index < tile_ranks[..., None]).astype(jnp.float32)
    return (tile_scales[:, 0] * tile_scales[:, 1])[..., None] * live_slots


def per_device_plain(
    left_factor, right_factor, tile_ranks, tile_scales, recorded, step_sizes, thresholds
):
    freqs_here = left_factor.shape[0]
    rows_here = left_factor.shape[1]
    col_tiles = left_factor.shape[2]
    rank_max = left_factor.shape[4]
    tile_width = left_factor.shape[5]
    row_tiles = right_factor.shape[1]
    cols_here = right_factor.shape[2]
    virtual = recorded.shape[2]
    tile_pos = lax.axis_index("tile")
    columns_here = cols_here * tile_width
    time_count = 2 * F
    highest = lax.Precision.HIGHEST
    weights = slot_weights(tile_ranks, tile_scales, rank_max)
    weights_right = lax.dynamic_slice_in_dim(weights, tile_pos * cols_here, cols_here, 2)
    weights_left = lax.dynamic_slice_in_dim(weights, tile_pos * rows_here, rows_here, 1)
    left_real = left_factor[:, :, :, 0]
    left_imag = left_factor[:, :, :, 1]
    right_real = right_factor[:, :, :, 0]
    right_imag = right_factor[:, :, :, 1]
    cos_all, sin_all = dft_tables(jnp.arange(F, dtype=jnp.int32), time_count)

    def gradient(residual):
        halves = residual.astype(jnp.bfloat16).reshape(
            freqs_here, 2, virtual, rows_here, tile_width
        )

        def contract_left(matrix, vectors):
            return jnp.einsum(
                "fijkq,fviq->fijkv", matrix, vectors, preferred_element_type=jnp.float32
            )

        dual_real = contract_left(left_real, halves[:, 0]) + contract_left(left_imag, halves[:, 1])
        dual_imag = contract_left(left_real, halves[:, 1]) - contract_left(left_imag, halves[:, 0])
        duals = (
            jnp.stack([dual_real, dual_imag], 3) * weights_left[:, :, :, None, :, None]
        ).astype(jnp.bfloat16)
        duals = duals.reshape(freqs_here, rows_here, col_tiles, 2, rank_max * virtual)
        arrived = lax.all_to_all(duals, "tile", split_axis=2, concat_axis=1, tiled=True)
        arrived = arrived.reshape(freqs_here, row_tiles, cols_here, 2, rank_max, virtual)

        def spread(matrix, vectors):
            return jnp.einsum(
                "fijkp,fijkv->fvjp", matrix, vectors, preferred_element_type=jnp.float32
            )

        grad_real = spread(right_real, arrived[:, :, :, 0]) - spread(
            right_imag, arrived[:, :, :, 1]
        )
        grad_imag = spread(right_real, arrived[:, :, :, 1]) + spread(
            right_imag, arrived[:, :, :, 0]
        )
        return jnp.stack([grad_real, grad_imag], 1).reshape(freqs_here, 2, virtual, columns_here)

    def to_time(wavefield):
        swapped = lax.all_to_all(wavefield, "freq", split_axis=3, concat_axis=0, tiled=True)
        return jnp.einsum("fvn,ft->nvt", swapped[:, 0], cos_all, precision=highest) - jnp.einsum(
            "fvn,ft->nvt", swapped[:, 1], sin_all, precision=highest
        )

    def shrink(signal):
        excess = jnp.abs(signal) - thresholds[None, :, None]
        return jnp.sign(signal) * jnp.maximum(excess, 0.0)

    def to_freq(signal):
        real_part = jnp.einsum("nvt,ft->fvn", signal, cos_all, precision=highest)
        imag_part = -jnp.einsum("nvt,ft->fvn", signal, sin_all, precision=highest)
        return lax.all_to_all(
            jnp.stack([real_part, imag_part], 1), "freq", split_axis=0, concat_axis=3, tiled=True
        )

    scaled = step_sizes[:, None, None, None]
    first = to_freq(shrink(to_time(scaled * gradient(recorded))))
    halves = first.astype(jnp.bfloat16).reshape(freqs_here, 2, virtual, cols_here, tile_width)

    def project(matrix, vectors):
        return jnp.einsum("fijkp,fvjp->fijkv", matrix, vectors, preferred_element_type=jnp.float32)

    coef_real = project(right_real, halves[:, 0]) + project(right_imag, halves[:, 1])
    coef_imag = project(right_real, halves[:, 1]) - project(right_imag, halves[:, 0])
    coeffs = (jnp.stack([coef_real, coef_imag], 3) * weights_right[:, :, :, None, :, None]).astype(
        jnp.bfloat16
    )
    coeffs = coeffs.reshape(freqs_here, row_tiles, cols_here, 2, rank_max * virtual)
    arrived = lax.all_to_all(coeffs, "tile", split_axis=1, concat_axis=2, tiled=True)
    arrived = arrived.reshape(freqs_here, rows_here, col_tiles, 2, rank_max, virtual)

    def expand(matrix, vectors):
        return jnp.einsum("fijkq,fijkv->fviq", matrix, vectors, preferred_element_type=jnp.float32)

    image_real = expand(left_real, arrived[:, :, :, 0]) - expand(left_imag, arrived[:, :, :, 1])
    image_imag = expand(left_real, arrived[:, :, :, 1]) + expand(left_imag, arrived[:, :, :, 0])
    return to_freq(
        shrink(
            to_time(
                first
                + scaled
                * gradient(
                    recorded
                    - jnp.stack([image_real, image_imag], 1).reshape(
                        freqs_here, 2, virtual, rows_here * tile_width
                    )
                )
            )
        )
    )


LANES = 128


def lane_ids(rows, lanes):
    return lax.broadcasted_iota(jnp.int32, (rows, lanes), 1)


def nt_dot(a, b):
    return lax.dot_general(a, b, (((1,), (1,)), ((), ())), preferred_element_type=jnp.float32)


def nn_dot(a, b):
    return jnp.dot(a, b, preferred_element_type=jnp.float32)


def swap(values):
    return pltpu.roll(values, LANES // 2, 1)


def part_sign(rows):
    return jnp.where(lane_ids(rows, LANES) < LANES // 2, 1.0, -1.0)


def split_two(values):
    high = values.astype(jnp.bfloat16)
    return high, (values - high.astype(jnp.float32)).astype(jnp.bfloat16)


def stacked_parts(ranks, scales):
    high = scales.astype(jnp.bfloat16)
    rest = scales - high.astype(jnp.float32)
    middle = rest.astype(jnp.bfloat16)
    low = (rest - middle.astype(jnp.float32)).astype(jnp.bfloat16)
    return high, middle, low, ranks.astype(jnp.float32).astype(jnp.bfloat16)


def weights_of(product, rows, rank):
    high, middle, low, ranks = [product[n * rows : (n + 1) * rows] for n in range(4)]
    slot = (lane_ids(rows, product.shape[1]) % rank).astype(jnp.float32)
    return jnp.where(slot < ranks - 0.5, high + middle + low, 0.0)


class Exchange:
    def __init__(self, axis, send, recv, send_sem, recv_sem):
        self.axis, self.send, self.recv = axis, send, recv
        self.send_sem, self.recv_sem = send_sem, recv_sem
        self.size = send.shape[2]
        self.me = lax.axis_index(axis)

    def peers(self):
        return [lax.rem(self.me + step, self.size) for step in range(1, self.size)]

    def start(self, half, block):
        for peer in self.peers():
            pltpu.make_async_remote_copy(
                src_ref=self.send.at[half, block, peer],
                dst_ref=self.recv.at[half, block, self.me],
                send_sem=self.send_sem,
                recv_sem=self.recv_sem.at[half, block],
                device_id={self.axis: peer},
                device_id_type=pl.DeviceIdType.MESH,
            ).start()
        self.recv[half, block, self.me] = self.send[half, block, self.me]

    def wait(self, half, block):
        others = pl.ds(0, self.size - 1)
        pltpu.make_async_remote_copy(
            src_ref=self.send.at[half, block, others],
            dst_ref=self.recv.at[half, block, others],
            send_sem=self.send_sem,
            recv_sem=self.recv_sem.at[half, block],
            device_id={self.axis: self.peers()[0]},
            device_id_type=pl.DeviceIdType.MESH,
        ).wait_recv()

    def finish(self):
        others = pl.ds(0, self.size - 1)
        pltpu.make_async_remote_copy(
            src_ref=self.send.at[:, :, others],
            dst_ref=self.recv.at[:, :, others],
            send_sem=self.send_sem,
            recv_sem=self.recv_sem.at[0, 0],
            device_id={self.axis: self.peers()[0]},
            device_id_type=pl.DeviceIdType.MESH,
        ).wait_send()


def whole_kernel(
    levels_ref, steps_ref, tables_hbm, left_hbm, right_hbm, recorded_hbm, ranks_hbm, scales_hbm,
    out_hbm,
    tables, left, right, recorded, ranks_ref, scales_ref, out_ref,
    left_sem, right_sem, small_sem, out_sem,
    weight_left, weight_right, residual, narrow, gathered, fields, kept,
    tile_send, tile_recv, freq_send, freq_recv, tile_ssem, tile_rsem, freq_ssem, freq_rsem,
):
    freqs, rows, tile_size, _, _, rank, width = left.shape
    row_tiles = right.shape[1]
    virtual = recorded.shape[2]
    per_half = LANES // (2 * rank)
    lanes_each = width // LANES
    halves, blocks = tile_send.shape[1:3]
    at_once = tile_send.shape[4]
    wide_blocks = freq_send.shape[2]
    wide_once = freqs // wide_blocks
    per_wide = wide_once // at_once
    both = 2 * virtual
    pieces = halves * blocks
    share = tile_size * LANES
    first_row = lax.axis_index("tile") * rows
    sign = part_sign(virtual)
    over_tile = [
        Exchange("tile", tile_send.at[n], tile_recv.at[n], tile_ssem.at[n], tile_rsem.at[n])
        for n in range(tile_send.shape[0])
    ]
    over_freq = [
        Exchange("freq", freq_send.at[n], freq_recv.at[n], freq_ssem.at[n], freq_rsem.at[n])
        for n in range(freq_send.shape[0])
    ]
    small = [
        pltpu.make_async_copy(source, target, small_sem.at[n])
        for n, (source, target) in enumerate(
            [(ranks_hbm, ranks_ref), (scales_hbm, scales_ref), (recorded_hbm, recorded),
             (tables_hbm, tables)]
        )
    ]

    def place(piece):
        return piece // blocks, piece % blocks

    def fetch_left(piece):
        half, block = place(piece)
        part = (pl.ds(block * at_once, at_once), slice(None), slice(None), pl.ds(half * per_half, per_half))
        return pltpu.make_async_copy(left_hbm.at[part], left.at[part], left_sem.at[half, block])

    def fetch_right(piece):
        half, block = place(piece)
        part = (pl.ds(block * at_once, at_once), slice(None), pl.ds(half * per_half, per_half))
        return pltpu.make_async_copy(right_hbm.at[part], right.at[part], right_sem.at[half, block])

    def each_freq(block, body):
        for inner in range(at_once):
            body(inner, block * at_once + inner)

    def left_rows(freq, row, half):
        own = pl.ds(half * per_half, per_half)
        return jnp.concatenate(
            [
                left[freq, row, tile, own, part].reshape(per_half * rank, width)
                for tile in range(tile_size)
                for part in range(2)
            ],
            0,
        )

    def dual(exchange, half, block, inner, freq, field_of):
        duals = []
        for row in range(rows):
            product = nt_dot(field_of(row), left_rows(freq, row, half))
            weight = weight_left[half, pl.ds(freq * row_tiles + first_row + row, 1), :]
            duals.append(
                [
                    (
                        product[:virtual, at : at + LANES] * sign
                        + swap(product[virtual:, at : at + LANES])
                    )
                    * weight[:, at : at + LANES]
                    for at in range(0, share, LANES)
                ]
            )
        for tile in range(tile_size):
            exchange.send[half, block, tile, inner] = jnp.concatenate(
                [duals[row][tile] for row in range(rows)], 0
            ).astype(jnp.bfloat16)

    def first_dual(piece):
        half, block = place(piece)

        def body(inner, freq):
            dual(
                over_tile[0], half, block, inner, freq,
                lambda row: recorded[freq, :, :, row * width : (row + 1) * width]
                .reshape(both, width)
                .astype(jnp.bfloat16),
            )

        each_freq(block, body)
        over_tile[0].start(half, block)

    owner = lane_ids(both, LANES) % (LANES // 2) // rank
    owns = [jnp.where(owner == n, 1.0, 0.0).astype(jnp.bfloat16) for n in range(per_half)]

    def spread(tiles, target, piece):
        half, block = place(piece)
        tiles.wait(half, block)
        own = pl.ds(half * per_half, per_half)

        def body(inner, freq):
            forms = []
            for tile in range(tile_size):
                arrived = tiles.recv[half, block, tile, inner].astype(jnp.float32)
                for row in range(rows):
                    part = arrived[row * virtual : (row + 1) * virtual]
                    forms.append(
                        jnp.concatenate([part * sign, swap(part)], 0).astype(jnp.bfloat16)
                    )
            matrix = jnp.concatenate(
                [jnp.concatenate([form * own_n for form in forms], 1) for own_n in owns], 0
            )
            factors = jnp.concatenate(
                [
                    right[freq, row, own, part].reshape(per_half * rank, width)
                    for row in range(row_tiles)
                    for part in range(2)
                ],
                0,
            )
            total = nn_dot(matrix, factors) * steps_ref[freq]
            within = (block % per_wide) * at_once + inner
            for col in range(per_half):
                for lane in range(lanes_each):
                    narrow[col * lanes_each + lane, pl.ds(within * both, both), :] = total[
                        col * both : (col + 1) * both, lane * LANES : (lane + 1) * LANES
                    ]

        each_freq(block, body)

        @pl.when(block % per_wide == per_wide - 1)
        def _():
            to = block // per_wide

            @pl.loop(0, per_half * lanes_each)
            def _(peer):
                for source in range(virtual):
                    target.send[half, to, peer, source] = narrow[
                        peer, pl.ds(source, 2 * wide_once, stride=virtual), :
                    ].astype(jnp.bfloat16)

            target.start(half, to)

    def shrink(second, source, target, half):
        for block in range(wide_blocks):
            source.wait(half, block)
        times = tables.shape[1]
        turn = jnp.where(
            lax.broadcasted_iota(jnp.int32, (times, 2 * LANES), 0) % 2 == 0, 1.0, -1.0
        )
        lane = lane_ids(1, 2 * LANES)
        for pair in range(virtual // 2):
            spectrum = jnp.concatenate(
                [
                    jnp.concatenate(
                        [
                            source.recv[half, block, peer, 2 * pair + n]
                            for peer in range(source.size)
                            for block in range(wide_blocks)
                        ],
                        0,
                    )
                    for n in range(2)
                ],
                1,
            )
            signal = nn_dot(tables[0], spectrum) + nn_dot(tables[1], spectrum)
            if second:
                signal += kept[half, pair]
            level = jnp.where(lane < LANES, levels_ref[2 * pair], levels_ref[2 * pair + 1])
            shrunk = signal - jnp.minimum(jnp.maximum(signal, -level), level)
            if not second:
                mean = jnp.sum(shrunk * turn, 0, keepdims=True) * (1.0 / times)
                kept[half, pair] = shrunk - turn * mean
            high, low = split_two(shrunk)
            back = (
                nn_dot(tables[2], high) + nn_dot(tables[3], high) + nn_dot(tables[2], low)
            ).astype(jnp.bfloat16)
            tall = 2 * wide_once
            for peer in range(target.size):
                for block in range(wide_blocks):
                    at = (peer * wide_blocks + block) * tall
                    for n in range(2):
                        target.send[half, block, peer, 2 * pair + n] = back[
                            at : at + tall, n * LANES : (n + 1) * LANES
                        ]
        for block in range(wide_blocks):
            target.start(half, block)

    def unshuffle(source, half, block, store):
        source.wait(half, block)
        tall = 2 * wide_once

        @pl.loop(0, source.size)
        def _(peer):
            for n in range(virtual):
                gathered[peer, n * tall : (n + 1) * tall] = source.recv[
                    half, block, peer, n
                ].astype(jnp.float32)

        @pl.loop(0, wide_once)
        def _(freq):
            for peer in range(source.size):
                store(
                    freq,
                    peer,
                    jnp.concatenate(
                        [
                            gathered[peer, pl.ds(2 * freq + part, virtual, stride=tall), :]
                            for part in range(2)
                        ],
                        0,
                    ).astype(jnp.bfloat16),
                )

    def store_field(freq, peer, values):
        fields[freq, :, peer * LANES : (peer + 1) * LANES] = values

    low_part = lane_ids(virtual, LANES) % (LANES // 2) < rows * rank

    def project(target, half, block):
        groups = row_tiles // per_half
        per_group = per_half // rows

        def body(inner, freq):
            within = (block % per_wide) * at_once + inner
            coefs = []
            for col in range(per_half):
                field = fields[within, :, col * width : (col + 1) * width]
                factors = jnp.concatenate(
                    [
                        right[
                            freq, group * per_half : (group + 1) * per_half,
                            half * per_half + col, part,
                        ].reshape(per_half * rank, width)
                        for group in range(groups)
                        for part in range(2)
                    ],
                    0,
                )
                product = nt_dot(field, factors)
                weight = weight_right[freq, pl.ds(half * per_half + col, 1), :]
                coefs.append(
                    [
                        (
                            product[:virtual, at : at + LANES] * sign
                            + swap(product[virtual:, at : at + LANES])
                        )
                        * weight[:, at : at + LANES]
                        for at in range(0, groups * LANES, LANES)
                    ]
                )
            shift = rows * rank
            for group in range(groups):
                lower, upper = [], []
                for col in range(0, per_half, per_group):
                    a, b = coefs[col][group], coefs[col + 1][group]
                    lower.append(jnp.where(low_part, a, pltpu.roll(b, shift, 1)))
                    upper.append(jnp.where(low_part, pltpu.roll(a, LANES - shift, 1), b))
                for n, packed in enumerate((lower, upper)):
                    target.send[half, block, group * per_group + n, inner] = jnp.concatenate(
                        packed, 0
                    ).astype(jnp.bfloat16)

        each_freq(block, body)
        target.start(half, block)

    row_owner = lane_ids(both, LANES) % (rows * rank) // rank
    row_owns = [jnp.where(row_owner == n, 1.0, 0.0).astype(jnp.bfloat16) for n in range(rows)]

    def image(source, half, block, inner, freq):
        per_group = per_half // rows
        forms = []
        for tile in range(tile_size):
            arrived = source.recv[half, block, tile, inner].astype(jnp.float32)
            for n in range(rows):
                part = arrived[n * virtual : (n + 1) * virtual]
                forms.append(jnp.concatenate([part * sign, swap(part)], 0).astype(jnp.bfloat16))
        matrix = jnp.concatenate(
            [jnp.concatenate([form * own for form in forms], 1) for own in row_owns], 0
        )
        factors = jnp.concatenate(
            [
                left[freq, row, tile, half * per_half + n * per_group + col, part]
                for tile in range(tile_size)
                for n in range(rows)
                for part in range(2)
                for col in range(per_group)
                for row in range(rows)
            ],
            0,
        )
        return nn_dot(matrix, factors)

    def first_image(block):
        over_tile[1].wait(0, block)

        def body(inner, freq):
            part = image(over_tile[1], 0, block, inner, freq)
            for row in range(rows):
                residual[freq, row] = (
                    recorded[freq, :, :, row * width : (row + 1) * width].reshape(both, width)
                    - part[row * both : (row + 1) * both]
                )

        each_freq(block, body)

    def last_image(block):
        over_tile[1].wait(1, block)

        def body(inner, freq):
            part = image(over_tile[1], 1, block, inner, freq)
            for row in range(rows):
                residual[freq, row] = residual[freq, row] - part[row * both : (row + 1) * both]

        each_freq(block, body)

    def last_dual(half, block):
        def body(inner, freq):
            dual(
                over_tile[2], half, block, inner, freq,
                lambda row: residual[freq, row].astype(jnp.bfloat16),
            )

        each_freq(block, body)
        over_tile[2].start(half, block)

    for copy in small[:2]:
        copy.start()
    for piece in range(AHEAD):
        fetch_left(piece).start()
        if piece == 0:
            small[2].start()

    barrier = pltpu.get_barrier_semaphore()
    count = 0
    for exchange in (over_tile[0], over_freq[0]):
        for peer in exchange.peers():
            pl.semaphore_signal(
                barrier, inc=1, device_id={exchange.axis: peer},
                device_id_type=pl.DeviceIdType.MESH,
            )
            count += 1

    for copy in small[:2]:
        copy.wait()
    tiles = ranks_ref.shape[2]
    lines = freqs * row_tiles
    parts = stacked_parts(
        ranks_ref[...].reshape(lines, tiles),
        (scales_ref[:, 0] * scales_ref[:, 1]).reshape(lines, tiles),
    )
    stacked = jnp.concatenate(parts, 0)
    for half in range(halves):
        lane = lane_ids(tiles, share)
        owner_tile = (
            lane // LANES * (halves * per_half) + half * per_half + lane % (LANES // 2) // rank
        )
        pick = jnp.where(
            owner_tile == lax.broadcasted_iota(jnp.int32, (tiles, share), 0), 1.0, 0.0
        ).astype(jnp.bfloat16)
        weight_left[half] = weights_of(nn_dot(stacked, pick), lines, rank)

    small[2].wait()
    pl.semaphore_wait(barrier, count)

    @pl.loop(0, pieces + TILE_LAG)
    def _(step):
        @pl.when(step + AHEAD < pieces)
        def _():
            fetch_left(step + AHEAD).start()

        @pl.when(step < pieces)
        def _():
            fetch_right(step).start()
            fetch_left(step).wait()
            first_dual(step)

        @pl.when(step == pieces - 1)
        def _():
            small[3].start()
            cols = weight_right.shape[1]
            mine = lax.axis_index("tile") * cols
            select = jnp.where(
                lane_ids(cols, tiles) == mine + lax.broadcasted_iota(jnp.int32, (cols, tiles), 0),
                1.0, 0.0,
            ).astype(jnp.bfloat16)
            turned = jnp.concatenate([nt_dot(select, part) for part in parts], 0).astype(
                jnp.bfloat16
            )
            lanes = weight_right.shape[2]
            lane = lane_ids(lines, lanes)
            owner_row = lane // LANES * per_half + lane % (LANES // 2) // rank

            @pl.loop(0, freqs)
            def _(freq):
                pick = jnp.where(
                    lax.broadcasted_iota(jnp.int32, (lines, lanes), 0)
                    == owner_row + freq * row_tiles,
                    1.0, 0.0,
                ).astype(jnp.bfloat16)
                weight_right[freq] = weights_of(nn_dot(turned, pick), cols, rank)

            small[3].wait()

        @pl.when(step >= TILE_LAG)
        def _():
            piece = step - TILE_LAG
            fetch_right(piece).wait()
            spread(over_tile[0], over_freq[0], piece)

    @pl.loop(0, halves)
    def _(half):
        shrink(False, over_freq[0], over_freq[1], half)

    @pl.loop(0, halves * wide_blocks)
    def _(step):
        half, block = step // wide_blocks, step % wide_blocks
        unshuffle(over_freq[1], half, block, store_field)

        @pl.loop(0, per_wide)
        def _(n):
            project(over_tile[1], half, block * per_wide + n)

        @pl.when(half == halves - 1)
        def _():
            @pl.loop(0, per_wide)
            def _(n):
                first_image(block * per_wide + n)

    @pl.loop(0, pieces + SECOND_LAG)
    def _(step):
        half, block = place(step)

        @pl.when(half == 0)
        def _():
            last_image(block)

        @pl.when(step < pieces)
        def _():
            last_dual(half, block)

        @pl.when(step >= SECOND_LAG)
        def _():
            spread(over_tile[2], over_freq[2], step - SECOND_LAG)

    @pl.loop(0, halves)
    def _(half):
        shrink(True, over_freq[2], over_freq[3], half)

    half_width = per_half * width

    def put(half, block):
        part = (
            pl.ds(block * wide_once, wide_once), slice(None), pl.ds(half * half_width, half_width)
        )
        return pltpu.make_async_copy(out_ref.at[half, block], out_hbm.at[part], out_sem.at[half, block])

    @pl.loop(0, halves * wide_blocks)
    def _(step):
        half, block = step // wide_blocks, step % wide_blocks

        def store(freq, peer, values):
            out_ref[half, block, freq, :, peer * LANES : (peer + 1) * LANES] = values

        unshuffle(over_freq[3], half, block, store)
        put(half, block).start()

    for half in range(halves):
        for block in range(wide_blocks):
            put(half, block).wait()
    for exchange in over_tile + over_freq:
        exchange.finish()


AHEAD = 3
TILE_LAG = 3
SECOND_LAG = 3


def table_parts():
    times = 2 * F
    freq = np.arange(F)[:, None]
    angles = (freq * np.arange(times)[None, :] % times) * (2.0 * math.pi / times)
    scaling = np.where(freq == 0, math.sqrt(1.0 / times), math.sqrt(2.0 / times))
    table = np.stack([scaling * np.cos(angles), -scaling * np.sin(angles)], 1)
    table = table.reshape(2 * F, times).astype(np.float32)
    high = table.astype(jnp.bfloat16)
    low = (table - high.astype(np.float32)).astype(jnp.bfloat16)
    return jnp.asarray(np.stack([high.T, low.T, high, low]))


def vmem():
    return pl.BlockSpec(memory_space=pltpu.VMEM)


def smem():
    return pl.BlockSpec(memory_space=pltpu.SMEM)


def per_device(
    left_factor, right_factor, tile_ranks, tile_scales, recorded, step_sizes, thresholds
):
    freqs, rows_here, col_tiles, _, rank, width = left_factor.shape
    row_tiles, cols_here = right_factor.shape[1:3]
    virtual = recorded.shape[2]
    tile_size = col_tiles // cols_here
    freq_size = lax.axis_size("freq")
    per_half = LANES // (2 * rank)
    halves = cols_here // per_half
    wide_once = 8
    wide_blocks = freqs // wide_once
    at_once = 4
    blocks = freqs // at_once
    both = 2 * virtual
    left_factor = left_factor.reshape(freqs, rows_here, tile_size, cols_here, 2, rank, width)
    out_shape = (freqs, both, cols_here * width)
    dma = pltpu.SemaphoreType.DMA
    tables = table_parts()
    bf16, f32 = jnp.bfloat16, jnp.float32
    tile_buffer = pltpu.VMEM(
        (3, halves, blocks, tile_size, at_once, rows_here * virtual, LANES), bf16
    )
    freq_buffer = pltpu.VMEM(
        (4, halves, wide_blocks, freq_size, virtual, 2 * wide_once, LANES), bf16
    )
    estimate = pl.pallas_call(
        whole_kernel,
        out_shape=jax.ShapeDtypeStruct(out_shape, bf16),
        in_specs=[smem(), smem()] + [pl.BlockSpec(memory_space=pl.ANY)] * 6,
        out_specs=pl.BlockSpec(memory_space=pl.ANY),
        scratch_shapes=[
            pltpu.VMEM(tables.shape, bf16),
            pltpu.VMEM(left_factor.shape, bf16),
            pltpu.VMEM(right_factor.shape, bf16),
            pltpu.VMEM(recorded.shape, f32),
            pltpu.VMEM(tile_ranks.shape, jnp.int32),
            pltpu.VMEM(tile_scales.shape, f32),
            pltpu.VMEM((halves, wide_blocks, wide_once, both, per_half * width), bf16),
            dma((halves, blocks)),
            dma((halves, blocks)),
            dma((4,)),
            dma((halves, wide_blocks)),
            pltpu.VMEM((halves, freqs * row_tiles, tile_size * LANES), f32),
            pltpu.VMEM((freqs, cols_here, row_tiles * 2 * rank), f32),
            pltpu.VMEM((freqs, rows_here, both, width), f32),
            pltpu.VMEM((freq_size, wide_once * both, LANES), f32),
            pltpu.VMEM((freq_size, wide_once * both, LANES), f32),
            pltpu.VMEM((wide_once, both, per_half * width), bf16),
            pltpu.VMEM((halves, virtual // 2, 2 * F, 2 * LANES), f32),
            tile_buffer,
            tile_buffer,
            freq_buffer,
            freq_buffer,
            dma((3,)),
            dma((3, halves, blocks)),
            dma((4,)),
            dma((4, halves, wide_blocks)),
        ],
        compiler_params=pltpu.CompilerParams(
            vmem_limit_bytes=58 << 20,
            collective_id=0,
            has_side_effects=True,
        ),
    )(
        thresholds, step_sizes, tables, left_factor, right_factor, recorded, tile_ranks,
        tile_scales,
    )
    return estimate.astype(jnp.float32).reshape(freqs, 2, virtual, cols_here * width)


def either(*arrays):
    left_factor, right_factor = arrays[:2]
    freqs, rows_here, col_tiles = left_factor.shape[:3]
    row_tiles, cols_here = right_factor.shape[1:3]
    rank, width = left_factor.shape[4:]
    freq_size = lax.axis_size("freq")
    aligned = (
        rank == 16
        and rows_here == 2
        and width % LANES == 0
        and cols_here == 2 * (LANES // (2 * rank))
        and freq_size == LANES // (2 * rank) * (width // LANES)
        and row_tiles % (LANES // (2 * rank)) == 0
        and row_tiles == rows_here * lax.axis_size("tile")
        and col_tiles == cols_here * lax.axis_size("tile")
        and arrays[4].shape[2] == 8
        and freqs % 8 == 0
        and freqs * freq_size == F
    )
    return (per_device if aligned else per_device_plain)(*arrays)


def solution(mesh):
    return jax.shard_map(
        either,
        mesh=mesh,
        in_specs=(
            P("freq", "tile", None, None, None, None),
            P("freq", None, "tile", None, None, None),
            P("freq", None, None),
            P("freq", None, None, None),
            P("freq", None, None, "tile"),
            P("freq"),
            P(),
        ),
        out_specs=P("freq", None, None, "tile"),
        check_vma=False,
    )
```

```python
import functools
import math

import jax
import jax.numpy as jnp
import numpy as np
from jax import lax
from jax.experimental import pallas as pl
from jax.experimental.pallas import tpu as pltpu
from jax.sharding import PartitionSpec as P

F = 128


def dft_tables(freq_index, time_count):
    times_row = jnp.arange(time_count, dtype=jnp.int32)
    phase_steps = (freq_index[:, None] * times_row[None, :] % time_count).astype(jnp.float32)
    angles = phase_steps * (2.0 * math.pi / time_count)
    scaling = jnp.where(
        freq_index == 0, math.sqrt(1.0 / time_count), math.sqrt(2.0 / time_count)
    ).astype(jnp.float32)
    return (scaling[:, None] * jnp.cos(angles), scaling[:, None] * jnp.sin(angles))


def slot_weights(tile_ranks, tile_scales, rank_max):
    slot_index = jnp.arange(rank_max, dtype=jnp.int32)
    live_slots = (slot_index < tile_ranks[..., None]).astype(jnp.float32)
    return (tile_scales[:, 0] * tile_scales[:, 1])[..., None] * live_slots


def per_device_plain(
    left_factor, right_factor, tile_ranks, tile_scales, recorded, step_sizes, thresholds
):
    freqs_here = left_factor.shape[0]
    rows_here = left_factor.shape[1]
    col_tiles = left_factor.shape[2]
    rank_max = left_factor.shape[4]
    tile_width = left_factor.shape[5]
    row_tiles = right_factor.shape[1]
    cols_here = right_factor.shape[2]
    virtual = recorded.shape[2]
    tile_pos = lax.axis_index("tile")
    columns_here = cols_here * tile_width
    time_count = 2 * F
    highest = lax.Precision.HIGHEST
    weights = slot_weights(tile_ranks, tile_scales, rank_max)
    weights_right = lax.dynamic_slice_in_dim(weights, tile_pos * cols_here, cols_here, 2)
    weights_left = lax.dynamic_slice_in_dim(weights, tile_pos * rows_here, rows_here, 1)
    left_real = left_factor[:, :, :, 0]
    left_imag = left_factor[:, :, :, 1]
    right_real = right_factor[:, :, :, 0]
    right_imag = right_factor[:, :, :, 1]
    cos_all, sin_all = dft_tables(jnp.arange(F, dtype=jnp.int32), time_count)

    def gradient(residual):
        halves = residual.astype(jnp.bfloat16).reshape(
            freqs_here, 2, virtual, rows_here, tile_width
        )

        def contract_left(matrix, vectors):
            return jnp.einsum(
                "fijkq,fviq->fijkv", matrix, vectors, preferred_element_type=jnp.float32
            )

        dual_real = contract_left(left_real, halves[:, 0]) + contract_left(left_imag, halves[:, 1])
        dual_imag = contract_left(left_real, halves[:, 1]) - contract_left(left_imag, halves[:, 0])
        duals = (
            jnp.stack([dual_real, dual_imag], 3) * weights_left[:, :, :, None, :, None]
        ).astype(jnp.bfloat16)
        duals = duals.reshape(freqs_here, rows_here, col_tiles, 2, rank_max * virtual)
        arrived = lax.all_to_all(duals, "tile", split_axis=2, concat_axis=1, tiled=True)
        arrived = arrived.reshape(freqs_here, row_tiles, cols_here, 2, rank_max, virtual)

        def spread(matrix, vectors):
            return jnp.einsum(
                "fijkp,fijkv->fvjp", matrix, vectors, preferred_element_type=jnp.float32
            )

        grad_real = spread(right_real, arrived[:, :, :, 0]) - spread(
            right_imag, arrived[:, :, :, 1]
        )
        grad_imag = spread(right_real, arrived[:, :, :, 1]) + spread(
            right_imag, arrived[:, :, :, 0]
        )
        return jnp.stack([grad_real, grad_imag], 1).reshape(freqs_here, 2, virtual, columns_here)

    def to_time(wavefield):
        swapped = lax.all_to_all(wavefield, "freq", split_axis=3, concat_axis=0, tiled=True)
        return jnp.einsum("fvn,ft->nvt", swapped[:, 0], cos_all, precision=highest) - jnp.einsum(
            "fvn,ft->nvt", swapped[:, 1], sin_all, precision=highest
        )

    def shrink(signal):
        excess = jnp.abs(signal) - thresholds[None, :, None]
        return jnp.sign(signal) * jnp.maximum(excess, 0.0)

    def to_freq(signal):
        real_part = jnp.einsum("nvt,ft->fvn", signal, cos_all, precision=highest)
        imag_part = -jnp.einsum("nvt,ft->fvn", signal, sin_all, precision=highest)
        return lax.all_to_all(
            jnp.stack([real_part, imag_part], 1), "freq", split_axis=0, concat_axis=3, tiled=True
        )

    scaled = step_sizes[:, None, None, None]
    first = to_freq(shrink(to_time(scaled * gradient(recorded))))
    halves = first.astype(jnp.bfloat16).reshape(freqs_here, 2, virtual, cols_here, tile_width)

    def project(matrix, vectors):
        return jnp.einsum("fijkp,fvjp->fijkv", matrix, vectors, preferred_element_type=jnp.float32)

    coef_real = project(right_real, halves[:, 0]) + project(right_imag, halves[:, 1])
    coef_imag = project(right_real, halves[:, 1]) - project(right_imag, halves[:, 0])
    coeffs = (jnp.stack([coef_real, coef_imag], 3) * weights_right[:, :, :, None, :, None]).astype(
        jnp.bfloat16
    )
    coeffs = coeffs.reshape(freqs_here, row_tiles, cols_here, 2, rank_max * virtual)
    arrived = lax.all_to_all(coeffs, "tile", split_axis=1, concat_axis=2, tiled=True)
    arrived = arrived.reshape(freqs_here, rows_here, col_tiles, 2, rank_max, virtual)

    def expand(matrix, vectors):
        return jnp.einsum("fijkq,fijkv->fviq", matrix, vectors, preferred_element_type=jnp.float32)

    image_real = expand(left_real, arrived[:, :, :, 0]) - expand(left_imag, arrived[:, :, :, 1])
    image_imag = expand(left_real, arrived[:, :, :, 1]) + expand(left_imag, arrived[:, :, :, 0])
    return to_freq(
        shrink(
            to_time(
                first
                + scaled
                * gradient(
                    recorded
                    - jnp.stack([image_real, image_imag], 1).reshape(
                        freqs_here, 2, virtual, rows_here * tile_width
                    )
                )
            )
        )
    )


LANES = 128


def lane_ids(rows, lanes):
    return lax.broadcasted_iota(jnp.int32, (rows, lanes), 1)


def nt_dot(a, b):
    return lax.dot_general(a, b, (((1,), (1,)), ((), ())), preferred_element_type=jnp.float32)


def nn_dot(a, b):
    return jnp.dot(a, b, preferred_element_type=jnp.float32)


def swap(values):
    return pltpu.roll(values, LANES // 2, 1)


def part_sign(rows):
    return jnp.where(lane_ids(rows, LANES) < LANES // 2, 1.0, -1.0)


def split_two(values):
    high = values.astype(jnp.bfloat16)
    return high, (values - high.astype(jnp.float32)).astype(jnp.bfloat16)


def stacked_parts(ranks, scales):
    high = scales.astype(jnp.bfloat16)
    rest = scales - high.astype(jnp.float32)
    middle = rest.astype(jnp.bfloat16)
    low = (rest - middle.astype(jnp.float32)).astype(jnp.bfloat16)
    return high, middle, low, ranks.astype(jnp.float32).astype(jnp.bfloat16)


def weights_of(product, rows, rank):
    high, middle, low, ranks = [product[n * rows : (n + 1) * rows] for n in range(4)]
    slot = (lane_ids(rows, product.shape[1]) % rank).astype(jnp.float32)
    return jnp.where(slot < ranks - 0.5, high + middle + low, 0.0)


class Exchange:
    def __init__(self, axis, send, recv, send_sem, recv_sem):
        self.axis, self.send, self.recv = axis, send, recv
        self.send_sem, self.recv_sem = send_sem, recv_sem
        self.size = send.shape[2]
        self.me = lax.axis_index(axis)

    def peers(self):
        return [lax.rem(self.me + step, self.size) for step in range(1, self.size)]

    def start(self, half, block):
        for peer in self.peers():
            pltpu.make_async_remote_copy(
                src_ref=self.send.at[half, block, peer],
                dst_ref=self.recv.at[half, block, self.me],
                send_sem=self.send_sem,
                recv_sem=self.recv_sem.at[half, block],
                device_id={self.axis: peer},
                device_id_type=pl.DeviceIdType.MESH,
            ).start()
        self.recv[half, block, self.me] = self.send[half, block, self.me]

    def wait(self, half, block):
        others = pl.ds(0, self.size - 1)
        pltpu.make_async_remote_copy(
            src_ref=self.send.at[half, block, others],
            dst_ref=self.recv.at[half, block, others],
            send_sem=self.send_sem,
            recv_sem=self.recv_sem.at[half, block],
            device_id={self.axis: self.peers()[0]},
            device_id_type=pl.DeviceIdType.MESH,
        ).wait_recv()

    def finish(self):
        others = pl.ds(0, self.size - 1)
        pltpu.make_async_remote_copy(
            src_ref=self.send.at[:, :, others],
            dst_ref=self.recv.at[:, :, others],
            send_sem=self.send_sem,
            recv_sem=self.recv_sem.at[0, 0],
            device_id={self.axis: self.peers()[0]},
            device_id_type=pl.DeviceIdType.MESH,
        ).wait_send()


def whole_kernel(
    levels_ref, steps_ref, tables_hbm, left_hbm, right_hbm, recorded_hbm, ranks_hbm, scales_hbm,
    out_hbm,
    tables, left, right, recorded, ranks_ref, scales_ref, out_ref,
    left_sem, right_sem, small_sem, out_sem,
    weight_left, weight_right, residual, narrow, gathered, fields, kept,
    tile_send, tile_recv, freq_send, freq_recv, tile_ssem, tile_rsem, freq_ssem, freq_rsem,
):
    freqs, rows, tile_size, _, _, rank, width = left.shape
    row_tiles = right.shape[1]
    virtual = recorded.shape[2]
    per_half = LANES // (2 * rank)
    lanes_each = width // LANES
    halves, blocks = tile_send.shape[1:3]
    at_once = tile_send.shape[4]
    tall = 2 * at_once
    both = 2 * virtual
    pieces = halves * blocks
    share = tile_size * LANES
    first_row = lax.axis_index("tile") * rows
    sign = part_sign(virtual)
    over_tile = [
        Exchange("tile", tile_send.at[n], tile_recv.at[n], tile_ssem.at[n], tile_rsem.at[n])
        for n in range(tile_send.shape[0])
    ]
    over_freq = [
        Exchange("freq", freq_send.at[n], freq_recv.at[n], freq_ssem.at[n], freq_rsem.at[n])
        for n in range(freq_send.shape[0])
    ]
    small = [
        pltpu.make_async_copy(source, target, small_sem.at[n])
        for n, (source, target) in enumerate(
            [(ranks_hbm, ranks_ref), (scales_hbm, scales_ref), (recorded_hbm, recorded),
             (tables_hbm, tables)]
        )
    ]

    def place(piece):
        return piece // blocks, piece % blocks

    def fetch_left(piece):
        half, block = place(piece)
        part = (pl.ds(block * at_once, at_once), slice(None), slice(None), pl.ds(half * per_half, per_half))
        return pltpu.make_async_copy(left_hbm.at[part], left.at[part], left_sem.at[half, block])

    def fetch_right(piece):
        half, block = place(piece)
        part = (pl.ds(block * at_once, at_once), slice(None), pl.ds(half * per_half, per_half))
        return pltpu.make_async_copy(right_hbm.at[part], right.at[part], right_sem.at[half, block])

    def each_freq(block, body):
        for inner in range(at_once):
            body(inner, block * at_once + inner)

    def left_rows(freq, row, half):
        own = pl.ds(half * per_half, per_half)
        return jnp.concatenate(
            [
                left[freq, row, tile, own, part].reshape(per_half * rank, width)
                for tile in range(tile_size)
                for part in range(2)
            ],
            0,
        )

    def dual(exchange, half, block, inner, freq, field_of):
        duals = []
        for row in range(rows):
            product = nt_dot(field_of(row), left_rows(freq, row, half))
            weight = weight_left[half, pl.ds(freq * row_tiles + first_row + row, 1), :]
            duals.append(
                [
                    (
                        product[:virtual, at : at + LANES] * sign
                        + swap(product[virtual:, at : at + LANES])
                    )
                    * weight[:, at : at + LANES]
                    for at in range(0, share, LANES)
                ]
            )
        for tile in range(tile_size):
            exchange.send[half, block, tile, inner] = jnp.concatenate(
                [duals[row][tile] for row in range(rows)], 0
            ).astype(jnp.bfloat16)

    def first_dual(piece):
        half, block = place(piece)

        def body(inner, freq):
            dual(
                over_tile[0], half, block, inner, freq,
                lambda row: recorded[freq, :, :, row * width : (row + 1) * width]
                .reshape(both, width)
                .astype(jnp.bfloat16),
            )

        each_freq(block, body)

        @pl.when(piece == 0)
        def _():
            pl.semaphore_wait(barrier, count)

        over_tile[0].start(half, block)

    owner = lane_ids(both, LANES) % (LANES // 2) // rank
    owns = [jnp.where(owner == n, 1.0, 0.0).astype(jnp.bfloat16) for n in range(per_half)]

    def spread(tiles, target, piece):
        half, block = place(piece)
        tiles.wait(half, block)
        own = pl.ds(half * per_half, per_half)

        def body(inner, freq):
            forms = []
            for tile in range(tile_size):
                arrived = tiles.recv[half, block, tile, inner].astype(jnp.float32)
                for row in range(rows):
                    part = arrived[row * virtual : (row + 1) * virtual]
                    forms.append(
                        jnp.concatenate([part * sign, swap(part)], 0).astype(jnp.bfloat16)
                    )
            matrix = jnp.concatenate(
                [jnp.concatenate([form * own_n for form in forms], 1) for own_n in owns], 0
            )
            factors = jnp.concatenate(
                [
                    right[freq, row, own, part].reshape(per_half * rank, width)
                    for row in range(row_tiles)
                    for part in range(2)
                ],
                0,
            )
            total = nn_dot(matrix, factors) * steps_ref[freq]
            for col in range(per_half):
                for lane in range(lanes_each):
                    narrow[col * lanes_each + lane, inner * both : (inner + 1) * both] = total[
                        col * both : (col + 1) * both, lane * LANES : (lane + 1) * LANES
                    ]

        each_freq(block, body)
        for peer in range(per_half * lanes_each):
            for pair in range(virtual // 2):
                target.send[half, block, peer, pair] = jnp.concatenate(
                    [
                        narrow[peer, pl.ds(2 * pair + n, tall, stride=virtual), :]
                        for n in range(2)
                    ],
                    0,
                ).astype(jnp.bfloat16)
        target.start(half, block)

    def shrink(second, source, target, half):
        for block in range(blocks):
            source.wait(half, block)
        times = tables.shape[1]
        turn = jnp.where(
            lax.broadcasted_iota(jnp.int32, (times, 2 * LANES), 0) % 2 == 0, 1.0, -1.0
        )
        lane = lane_ids(1, 2 * LANES)
        for pair in range(virtual // 2):
            arrived = [
                source.recv[half, block, peer, pair].astype(jnp.float32)
                for peer in range(source.size)
                for block in range(blocks)
            ]
            spectrum = jnp.concatenate(
                [
                    jnp.concatenate([part[n * tall : (n + 1) * tall] for part in arrived], 0)
                    for n in range(2)
                ],
                1,
            ).astype(jnp.bfloat16)
            signal = nn_dot(tables[0], spectrum) + nn_dot(tables[1], spectrum)
            if second:
                signal += kept[half, pair]
            level = jnp.where(lane < LANES, levels_ref[2 * pair], levels_ref[2 * pair + 1])
            shrunk = signal - jnp.minimum(jnp.maximum(signal, -level), level)
            if not second:
                mean = jnp.sum(shrunk * turn, 0, keepdims=True) * (1.0 / times)
                kept[half, pair] = shrunk - turn * mean
            high, low = split_two(shrunk)
            back = nn_dot(tables[2], high) + nn_dot(tables[3], high) + nn_dot(tables[2], low)
            for peer in range(target.size):
                for block in range(blocks):
                    at = (peer * blocks + block) * tall
                    target.send[half, block, peer, pair] = jnp.concatenate(
                        [back[at : at + tall, n * LANES : (n + 1) * LANES] for n in range(2)], 0
                    ).astype(jnp.bfloat16)
        for block in range(blocks):
            target.start(half, block)

    def unshuffle(source, half, block, store):
        source.wait(half, block)
        for peer in range(source.size):
            for pair in range(virtual // 2):
                gathered[peer, pair * both : (pair + 1) * both] = source.recv[
                    half, block, peer, pair
                ].astype(jnp.float32)
        for freq in range(at_once):
            for peer in range(source.size):
                values = [
                    gathered[peer, pl.ds(2 * freq + part, virtual, stride=tall), :]
                    for part in range(2)
                ]
                store(freq, peer, jnp.concatenate(values, 0).astype(jnp.bfloat16))

    def store_field(freq, peer, values):
        fields[freq, :, peer * LANES : (peer + 1) * LANES] = values

    low_part = lane_ids(virtual, LANES) % (LANES // 2) < rows * rank

    def project(target, half, block):
        groups = row_tiles // per_half
        per_group = per_half // rows

        def body(inner, freq):
            coefs = []
            for col in range(per_half):
                field = fields[inner, :, col * width : (col + 1) * width]
                factors = jnp.concatenate(
                    [
                        right[
                            freq, group * per_half : (group + 1) * per_half,
                            half * per_half + col, part,
                        ].reshape(per_half * rank, width)
                        for group in range(groups)
                        for part in range(2)
                    ],
                    0,
                )
                product = nt_dot(field, factors)
                weight = weight_right[freq, pl.ds(half * per_half + col, 1), :]
                coefs.append(
                    [
                        (
                            product[:virtual, at : at + LANES] * sign
                            + swap(product[virtual:, at : at + LANES])
                        )
                        * weight[:, at : at + LANES]
                        for at in range(0, groups * LANES, LANES)
                    ]
                )
            shift = rows * rank
            for group in range(groups):
                lower, upper = [], []
                for col in range(0, per_half, per_group):
                    a, b = coefs[col][group], coefs[col + 1][group]
                    lower.append(jnp.where(low_part, a, pltpu.roll(b, shift, 1)))
                    upper.append(jnp.where(low_part, pltpu.roll(a, LANES - shift, 1), b))
                for n, packed in enumerate((lower, upper)):
                    target.send[half, block, group * per_group + n, inner] = jnp.concatenate(
                        packed, 0
                    ).astype(jnp.bfloat16)

        each_freq(block, body)
        target.start(half, block)

    row_owner = lane_ids(both, LANES) % (rows * rank) // rank
    row_owns = [jnp.where(row_owner == n, 1.0, 0.0).astype(jnp.bfloat16) for n in range(rows)]

    def image(source, half, block, inner, freq):
        per_group = per_half // rows
        forms = []
        for tile in range(tile_size):
            arrived = source.recv[half, block, tile, inner].astype(jnp.float32)
            for n in range(rows):
                part = arrived[n * virtual : (n + 1) * virtual]
                forms.append(jnp.concatenate([part * sign, swap(part)], 0).astype(jnp.bfloat16))
        matrix = jnp.concatenate(
            [jnp.concatenate([form * own for form in forms], 1) for own in row_owns], 0
        )
        factors = jnp.concatenate(
            [
                left[freq, row, tile, half * per_half + n * per_group + col, part]
                for tile in range(tile_size)
                for n in range(rows)
                for part in range(2)
                for col in range(per_group)
                for row in range(rows)
            ],
            0,
        )
        return nn_dot(matrix, factors)

    def first_image(block):
        over_tile[1].wait(0, block)

        def body(inner, freq):
            part = image(over_tile[1], 0, block, inner, freq)
            for row in range(rows):
                residual[freq, row] = (
                    recorded[freq, :, :, row * width : (row + 1) * width].reshape(both, width)
                    - part[row * both : (row + 1) * both]
                )

        each_freq(block, body)

    def last_image(block):
        over_tile[1].wait(1, block)

        def body(inner, freq):
            part = image(over_tile[1], 1, block, inner, freq)
            for row in range(rows):
                residual[freq, row] = residual[freq, row] - part[row * both : (row + 1) * both]

        each_freq(block, body)

    def last_dual(half, block):
        def body(inner, freq):
            dual(
                over_tile[2], half, block, inner, freq,
                lambda row: residual[freq, row].astype(jnp.bfloat16),
            )

        each_freq(block, body)
        over_tile[2].start(half, block)

    for copy in small[:2]:
        copy.start()
    for piece in range(AHEAD):
        fetch_left(piece).start()
        if piece == 0:
            small[2].start()

    barrier = pltpu.get_barrier_semaphore()
    count = 0
    for exchange in (over_tile[0], over_freq[0]):
        for peer in exchange.peers():
            pl.semaphore_signal(
                barrier, inc=1, device_id={exchange.axis: peer},
                device_id_type=pl.DeviceIdType.MESH,
            )
            count += 1

    for copy in small[:2]:
        copy.wait()
    tiles = ranks_ref.shape[2]
    lines = freqs * row_tiles
    parts = stacked_parts(
        ranks_ref[...].reshape(lines, tiles),
        (scales_ref[:, 0] * scales_ref[:, 1]).reshape(lines, tiles),
    )
    stacked = jnp.concatenate(parts, 0)
    for half in range(halves):
        lane = lane_ids(tiles, share)
        owner_tile = (
            lane // LANES * (halves * per_half) + half * per_half + lane % (LANES // 2) // rank
        )
        pick = jnp.where(
            owner_tile == lax.broadcasted_iota(jnp.int32, (tiles, share), 0), 1.0, 0.0
        ).astype(jnp.bfloat16)
        weight_left[half] = weights_of(nn_dot(stacked, pick), lines, rank)

    small[2].wait()

    @pl.loop(0, pieces + TILE_LAG)
    def _(step):
        @pl.when(step + AHEAD < pieces)
        def _():
            fetch_left(step + AHEAD).start()

        @pl.when(step < pieces)
        def _():
            fetch_right(step).start()
            fetch_left(step).wait()
            first_dual(step)

        @pl.when(step == pieces - 1)
        def _():
            small[3].start()
            cols = weight_right.shape[1]
            mine = lax.axis_index("tile") * cols
            select = jnp.where(
                lane_ids(cols, tiles) == mine + lax.broadcasted_iota(jnp.int32, (cols, tiles), 0),
                1.0, 0.0,
            ).astype(jnp.bfloat16)
            turned = jnp.concatenate([nt_dot(select, part) for part in parts], 0).astype(
                jnp.bfloat16
            )
            lanes = weight_right.shape[2]
            lane = lane_ids(lines, lanes)
            owner_row = lane // LANES * per_half + lane % (LANES // 2) // rank

            @pl.loop(0, freqs)
            def _(freq):
                pick = jnp.where(
                    lax.broadcasted_iota(jnp.int32, (lines, lanes), 0)
                    == owner_row + freq * row_tiles,
                    1.0, 0.0,
                ).astype(jnp.bfloat16)
                weight_right[freq] = weights_of(nn_dot(turned, pick), cols, rank)

            small[3].wait()

        @pl.when(step >= TILE_LAG)
        def _():
            piece = step - TILE_LAG
            fetch_right(piece).wait()
            spread(over_tile[0], over_freq[0], piece)

    @pl.loop(0, halves)
    def _(half):
        shrink(False, over_freq[0], over_freq[1], half)

    @pl.loop(0, pieces)
    def _(step):
        half, block = place(step)
        unshuffle(over_freq[1], half, block, store_field)
        project(over_tile[1], half, block)

        @pl.when(half == halves - 1)
        def _():
            first_image(block)

    @pl.loop(0, pieces + SECOND_LAG)
    def _(step):
        half, block = place(step)

        @pl.when(half == 0)
        def _():
            last_image(block)

        @pl.when(step < pieces)
        def _():
            last_dual(half, block)

        @pl.when(step >= SECOND_LAG)
        def _():
            spread(over_tile[2], over_freq[2], step - SECOND_LAG)

    @pl.loop(0, halves)
    def _(half):
        shrink(True, over_freq[2], over_freq[3], half)

    half_width = per_half * width

    def put(half, block):
        part = (
            pl.ds(block * at_once, at_once), slice(None), pl.ds(half * half_width, half_width)
        )
        return pltpu.make_async_copy(out_ref.at[half, block], out_hbm.at[part], out_sem.at[half, block])

    @pl.loop(0, pieces)
    def _(step):
        half, block = place(step)

        def store(freq, peer, values):
            out_ref[half, block, freq, :, peer * LANES : (peer + 1) * LANES] = values

        unshuffle(over_freq[3], half, block, store)
        put(half, block).start()

    for half in range(halves):
        for block in range(blocks):
            put(half, block).wait()
    for exchange in over_tile + over_freq:
        exchange.finish()


AHEAD = 3
TILE_LAG = 3
SECOND_LAG = 3


def table_parts():
    times = 2 * F
    freq = np.arange(F)[:, None]
    angles = (freq * np.arange(times)[None, :] % times) * (2.0 * math.pi / times)
    scaling = np.where(freq == 0, math.sqrt(1.0 / times), math.sqrt(2.0 / times))
    table = np.stack([scaling * np.cos(angles), -scaling * np.sin(angles)], 1)
    table = table.reshape(2 * F, times).astype(np.float32)
    high = table.astype(jnp.bfloat16)
    low = (table - high.astype(np.float32)).astype(jnp.bfloat16)
    return jnp.asarray(np.stack([high.T, low.T, high, low]))


def vmem():
    return pl.BlockSpec(memory_space=pltpu.VMEM)


def smem():
    return pl.BlockSpec(memory_space=pltpu.SMEM)


def per_device(
    left_factor, right_factor, tile_ranks, tile_scales, recorded, step_sizes, thresholds
):
    freqs, rows_here, col_tiles, _, rank, width = left_factor.shape
    row_tiles, cols_here = right_factor.shape[1:3]
    virtual = recorded.shape[2]
    tile_size = col_tiles // cols_here
    freq_size = lax.axis_size("freq")
    per_half = LANES // (2 * rank)
    halves = cols_here // per_half
    at_once = 4
    blocks = freqs // at_once
    both = 2 * virtual
    left_factor = left_factor.reshape(freqs, rows_here, tile_size, cols_here, 2, rank, width)
    out_shape = (freqs, both, cols_here * width)
    dma = pltpu.SemaphoreType.DMA
    tables = table_parts()
    bf16, f32 = jnp.bfloat16, jnp.float32
    tile_buffer = pltpu.VMEM(
        (3, halves, blocks, tile_size, at_once, rows_here * virtual, LANES), bf16
    )
    freq_buffer = pltpu.VMEM(
        (4, halves, blocks, freq_size, virtual // 2, 2 * 2 * at_once, LANES), bf16
    )
    estimate = pl.pallas_call(
        whole_kernel,
        out_shape=jax.ShapeDtypeStruct(out_shape, bf16),
        in_specs=[smem(), smem()] + [pl.BlockSpec(memory_space=pl.ANY)] * 6,
        out_specs=pl.BlockSpec(memory_space=pl.ANY),
        scratch_shapes=[
            pltpu.VMEM(tables.shape, bf16),
            pltpu.VMEM(left_factor.shape, bf16),
            pltpu.VMEM(right_factor.shape, bf16),
            pltpu.VMEM(recorded.shape, f32),
            pltpu.VMEM(tile_ranks.shape, jnp.int32),
            pltpu.VMEM(tile_scales.shape, f32),
            pltpu.VMEM((halves, blocks, at_once, both, per_half * width), bf16),
            dma((halves, blocks)),
            dma((halves, blocks)),
            dma((4,)),
            dma((halves, blocks)),
            pltpu.VMEM((halves, freqs * row_tiles, tile_size * LANES), f32),
            pltpu.VMEM((freqs, cols_here, row_tiles * 2 * rank), f32),
            pltpu.VMEM((freqs, rows_here, both, width), f32),
            pltpu.VMEM((freq_size, at_once * both, LANES), f32),
            pltpu.VMEM((freq_size, at_once * both, LANES), f32),
            pltpu.VMEM((at_once, both, per_half * width), bf16),
            pltpu.VMEM((halves, virtual // 2, 2 * F, 2 * LANES), f32),
            tile_buffer,
            tile_buffer,
            freq_buffer,
            freq_buffer,
            dma((3,)),
            dma((3, halves, blocks)),
            dma((4,)),
            dma((4, halves, blocks)),
        ],
        compiler_params=pltpu.CompilerParams(
            vmem_limit_bytes=58 << 20,
            collective_id=0,
            has_side_effects=True,
        ),
    )(
        thresholds, step_sizes, tables, left_factor, right_factor, recorded, tile_ranks,
        tile_scales,
    )
    return estimate.astype(jnp.float32).reshape(freqs, 2, virtual, cols_here * width)


def either(*arrays):
    left_factor, right_factor = arrays[:2]
    freqs, rows_here, col_tiles = left_factor.shape[:3]
    row_tiles, cols_here = right_factor.shape[1:3]
    rank, width = left_factor.shape[4:]
    freq_size = lax.axis_size("freq")
    aligned = (
        rank == 16
        and rows_here == 2
        and width % LANES == 0
        and cols_here == 2 * (LANES // (2 * rank))
        and freq_size == LANES // (2 * rank) * (width // LANES)
        and row_tiles % (LANES // (2 * rank)) == 0
        and row_tiles == rows_here * lax.axis_size("tile")
        and col_tiles == cols_here * lax.axis_size("tile")
        and arrays[4].shape[2] == 8
        and freqs % 8 == 0
        and freqs * freq_size == F
    )
    return (per_device if aligned else per_device_plain)(*arrays)


def solution(mesh):
    return jax.shard_map(
        either,
        mesh=mesh,
        in_specs=(
            P("freq", "tile", None, None, None, None),
            P("freq", None, "tile", None, None, None),
            P("freq", None, None),
            P("freq", None, None, None),
            P("freq", None, None, "tile"),
            P("freq"),
            P(),
        ),
        out_specs=P("freq", None, None, "tile"),
        check_vma=False,
    )
```

```python
import functools
import math

import jax
import jax.numpy as jnp
import numpy as np
from jax import lax
from jax.experimental import pallas as pl
from jax.experimental.pallas import tpu as pltpu
from jax.sharding import PartitionSpec as P

F = 128


def dft_tables(freq_index, time_count):
    times_row = jnp.arange(time_count, dtype=jnp.int32)
    phase_steps = (freq_index[:, None] * times_row[None, :] % time_count).astype(jnp.float32)
    angles = phase_steps * (2.0 * math.pi / time_count)
    scaling = jnp.where(
        freq_index == 0, math.sqrt(1.0 / time_count), math.sqrt(2.0 / time_count)
    ).astype(jnp.float32)
    return (scaling[:, None] * jnp.cos(angles), scaling[:, None] * jnp.sin(angles))


def slot_weights(tile_ranks, tile_scales, rank_max):
    slot_index = jnp.arange(rank_max, dtype=jnp.int32)
    live_slots = (slot_index < tile_ranks[..., None]).astype(jnp.float32)
    return (tile_scales[:, 0] * tile_scales[:, 1])[..., None] * live_slots


def per_device_plain(
    left_factor, right_factor, tile_ranks, tile_scales, recorded, step_sizes, thresholds
):
    freqs_here = left_factor.shape[0]
    rows_here = left_factor.shape[1]
    col_tiles = left_factor.shape[2]
    rank_max = left_factor.shape[4]
    tile_width = left_factor.shape[5]
    row_tiles = right_factor.shape[1]
    cols_here = right_factor.shape[2]
    virtual = recorded.shape[2]
    tile_pos = lax.axis_index("tile")
    columns_here = cols_here * tile_width
    time_count = 2 * F
    highest = lax.Precision.HIGHEST
    weights = slot_weights(tile_ranks, tile_scales, rank_max)
    weights_right = lax.dynamic_slice_in_dim(weights, tile_pos * cols_here, cols_here, 2)
    weights_left = lax.dynamic_slice_in_dim(weights, tile_pos * rows_here, rows_here, 1)
    left_real = left_factor[:, :, :, 0]
    left_imag = left_factor[:, :, :, 1]
    right_real = right_factor[:, :, :, 0]
    right_imag = right_factor[:, :, :, 1]
    cos_all, sin_all = dft_tables(jnp.arange(F, dtype=jnp.int32), time_count)

    def gradient(residual):
        halves = residual.astype(jnp.bfloat16).reshape(
            freqs_here, 2, virtual, rows_here, tile_width
        )

        def contract_left(matrix, vectors):
            return jnp.einsum(
                "fijkq,fviq->fijkv", matrix, vectors, preferred_element_type=jnp.float32
            )

        dual_real = contract_left(left_real, halves[:, 0]) + contract_left(left_imag, halves[:, 1])
        dual_imag = contract_left(left_real, halves[:, 1]) - contract_left(left_imag, halves[:, 0])
        duals = (
            jnp.stack([dual_real, dual_imag], 3) * weights_left[:, :, :, None, :, None]
        ).astype(jnp.bfloat16)
        duals = duals.reshape(freqs_here, rows_here, col_tiles, 2, rank_max * virtual)
        arrived = lax.all_to_all(duals, "tile", split_axis=2, concat_axis=1, tiled=True)
        arrived = arrived.reshape(freqs_here, row_tiles, cols_here, 2, rank_max, virtual)

        def spread(matrix, vectors):
            return jnp.einsum(
                "fijkp,fijkv->fvjp", matrix, vectors, preferred_element_type=jnp.float32
            )

        grad_real = spread(right_real, arrived[:, :, :, 0]) - spread(
            right_imag, arrived[:, :, :, 1]
        )
        grad_imag = spread(right_real, arrived[:, :, :, 1]) + spread(
            right_imag, arrived[:, :, :, 0]
        )
        return jnp.stack([grad_real, grad_imag], 1).reshape(freqs_here, 2, virtual, columns_here)

    def to_time(wavefield):
        swapped = lax.all_to_all(wavefield, "freq", split_axis=3, concat_axis=0, tiled=True)
        return jnp.einsum("fvn,ft->nvt", swapped[:, 0], cos_all, precision=highest) - jnp.einsum(
            "fvn,ft->nvt", swapped[:, 1], sin_all, precision=highest
        )

    def shrink(signal):
        excess = jnp.abs(signal) - thresholds[None, :, None]
        return jnp.sign(signal) * jnp.maximum(excess, 0.0)

    def to_freq(signal):
        real_part = jnp.einsum("nvt,ft->fvn", signal, cos_all, precision=highest)
        imag_part = -jnp.einsum("nvt,ft->fvn", signal, sin_all, precision=highest)
        return lax.all_to_all(
            jnp.stack([real_part, imag_part], 1), "freq", split_axis=0, concat_axis=3, tiled=True
        )

    scaled = step_sizes[:, None, None, None]
    first = to_freq(shrink(to_time(scaled * gradient(recorded))))
    halves = first.astype(jnp.bfloat16).reshape(freqs_here, 2, virtual, cols_here, tile_width)

    def project(matrix, vectors):
        return jnp.einsum("fijkp,fvjp->fijkv", matrix, vectors, preferred_element_type=jnp.float32)

    coef_real = project(right_real, halves[:, 0]) + project(right_imag, halves[:, 1])
    coef_imag = project(right_real, halves[:, 1]) - project(right_imag, halves[:, 0])
    coeffs = (jnp.stack([coef_real, coef_imag], 3) * weights_right[:, :, :, None, :, None]).astype(
        jnp.bfloat16
    )
    coeffs = coeffs.reshape(freqs_here, row_tiles, cols_here, 2, rank_max * virtual)
    arrived = lax.all_to_all(coeffs, "tile", split_axis=1, concat_axis=2, tiled=True)
    arrived = arrived.reshape(freqs_here, rows_here, col_tiles, 2, rank_max, virtual)

    def expand(matrix, vectors):
        return jnp.einsum("fijkq,fijkv->fviq", matrix, vectors, preferred_element_type=jnp.float32)

    image_real = expand(left_real, arrived[:, :, :, 0]) - expand(left_imag, arrived[:, :, :, 1])
    image_imag = expand(left_real, arrived[:, :, :, 1]) + expand(left_imag, arrived[:, :, :, 0])
    return to_freq(
        shrink(
            to_time(
                first
                + scaled
                * gradient(
                    recorded
                    - jnp.stack([image_real, image_imag], 1).reshape(
                        freqs_here, 2, virtual, rows_here * tile_width
                    )
                )
            )
        )
    )


LANES = 128


def lane_ids(rows, lanes):
    return lax.broadcasted_iota(jnp.int32, (rows, lanes), 1)


def nt_dot(a, b):
    return lax.dot_general(a, b, (((1,), (1,)), ((), ())), preferred_element_type=jnp.float32)


def nn_dot(a, b):
    return jnp.dot(a, b, preferred_element_type=jnp.float32)


def swap(values):
    return pltpu.roll(values, LANES // 2, 1)


def part_sign(rows):
    return jnp.where(lane_ids(rows, LANES) < LANES // 2, 1.0, -1.0)


def split_two(values):
    high = values.astype(jnp.bfloat16)
    return high, (values - high.astype(jnp.float32)).astype(jnp.bfloat16)


def stacked_parts(ranks, scales):
    high = scales.astype(jnp.bfloat16)
    rest = scales - high.astype(jnp.float32)
    middle = rest.astype(jnp.bfloat16)
    low = (rest - middle.astype(jnp.float32)).astype(jnp.bfloat16)
    return high, middle, low, ranks.astype(jnp.float32).astype(jnp.bfloat16)


def weights_of(product, rows, rank):
    high, middle, low, ranks = [product[n * rows : (n + 1) * rows] for n in range(4)]
    slot = (lane_ids(rows, product.shape[1]) % rank).astype(jnp.float32)
    return jnp.where(slot < ranks - 0.5, high + middle + low, 0.0)


class Exchange:
    def __init__(self, axis, send, recv, send_sem, recv_sem):
        self.axis, self.send, self.recv = axis, send, recv
        self.send_sem, self.recv_sem = send_sem, recv_sem
        self.size = send.shape[2]
        self.me = lax.axis_index(axis)

    def peers(self):
        return [lax.rem(self.me + step, self.size) for step in range(1, self.size)]

    def start(self, half, block):
        for peer in self.peers():
            pltpu.make_async_remote_copy(
                src_ref=self.send.at[half, block, peer],
                dst_ref=self.recv.at[half, block, self.me],
                send_sem=self.send_sem,
                recv_sem=self.recv_sem.at[half, block],
                device_id={self.axis: peer},
                device_id_type=pl.DeviceIdType.MESH,
            ).start()
        self.recv[half, block, self.me] = self.send[half, block, self.me]

    def wait(self, half, block):
        others = pl.ds(0, self.size - 1)
        pltpu.make_async_remote_copy(
            src_ref=self.send.at[half, block, others],
            dst_ref=self.recv.at[half, block, others],
            send_sem=self.send_sem,
            recv_sem=self.recv_sem.at[half, block],
            device_id={self.axis: self.peers()[0]},
            device_id_type=pl.DeviceIdType.MESH,
        ).wait_recv()

    def finish(self):
        others = pl.ds(0, self.size - 1)
        pltpu.make_async_remote_copy(
            src_ref=self.send.at[:, :, others],
            dst_ref=self.recv.at[:, :, others],
            send_sem=self.send_sem,
            recv_sem=self.recv_sem.at[0, 0],
            device_id={self.axis: self.peers()[0]},
            device_id_type=pl.DeviceIdType.MESH,
        ).wait_send()


def whole_kernel(
    levels_ref, steps_ref, tables_hbm, left_hbm, right_hbm, recorded_hbm, ranks_hbm, scales_hbm,
    out_hbm,
    tables, left, right, recorded, ranks_ref, scales_ref, out_ref,
    left_sem, right_sem, small_sem, out_sem,
    weight_left, weight_right, residual, narrow, gathered, fields, kept,
    tile_send, tile_recv, freq_send, freq_recv, tile_ssem, tile_rsem, freq_ssem, freq_rsem,
):
    freqs, rows, tile_size, _, _, rank, width = left.shape
    row_tiles = right.shape[1]
    virtual = recorded.shape[2]
    per_half = LANES // (2 * rank)
    lanes_each = width // LANES
    halves, blocks = tile_send.shape[1:3]
    at_once = tile_send.shape[4]
    tall = 2 * at_once
    both = 2 * virtual
    pieces = halves * blocks
    share = tile_size * LANES
    first_row = lax.axis_index("tile") * rows
    sign = part_sign(virtual)
    over_tile = [
        Exchange("tile", tile_send.at[n], tile_recv.at[n], tile_ssem.at[n], tile_rsem.at[n])
        for n in range(tile_send.shape[0])
    ]
    over_freq = [
        Exchange("freq", freq_send.at[n], freq_recv.at[n], freq_ssem.at[n], freq_rsem.at[n])
        for n in range(freq_send.shape[0])
    ]
    small = [
        pltpu.make_async_copy(source, target, small_sem.at[n])
        for n, (source, target) in enumerate(
            [(ranks_hbm, ranks_ref), (scales_hbm, scales_ref), (recorded_hbm, recorded),
             (tables_hbm, tables)]
        )
    ]

    def place(piece):
        return piece // blocks, piece % blocks

    def fetch_left(piece):
        half, block = place(piece)
        part = (pl.ds(block * at_once, at_once), slice(None), slice(None), pl.ds(half * per_half, per_half))
        return pltpu.make_async_copy(left_hbm.at[part], left.at[part], left_sem.at[half, block])

    def fetch_right(piece):
        half, block = place(piece)
        part = (pl.ds(block * at_once, at_once), slice(None), pl.ds(half * per_half, per_half))
        return pltpu.make_async_copy(right_hbm.at[part], right.at[part], right_sem.at[half, block])

    def each_freq(block, body):
        for inner in range(at_once):
            body(inner, block * at_once + inner)

    def left_rows(freq, row, half):
        own = pl.ds(half * per_half, per_half)
        return jnp.concatenate(
            [
                left[freq, row, tile, own, part].reshape(per_half * rank, width)
                for tile in range(tile_size)
                for part in range(2)
            ],
            0,
        )

    def dual(exchange, half, block, inner, freq, field_of):
        duals = []
        for row in range(rows):
            product = nt_dot(field_of(row), left_rows(freq, row, half))
            weight = weight_left[half, pl.ds(freq * row_tiles + first_row + row, 1), :]
            duals.append(
                [
                    (
                        product[:virtual, at : at + LANES] * sign
                        + swap(product[virtual:, at : at + LANES])
                    )
                    * weight[:, at : at + LANES]
                    for at in range(0, share, LANES)
                ]
            )
        for tile in range(tile_size):
            exchange.send[half, block, tile, inner] = jnp.concatenate(
                [duals[row][tile] for row in range(rows)], 0
            ).astype(jnp.bfloat16)

    def first_dual(piece):
        half, block = place(piece)

        def body(inner, freq):
            dual(
                over_tile[0], half, block, inner, freq,
                lambda row: recorded[freq, :, :, row * width : (row + 1) * width]
                .reshape(both, width)
                .astype(jnp.bfloat16),
            )

        each_freq(block, body)

        @pl.when(piece == 0)
        def _():
            pl.semaphore_wait(barrier, count)

        over_tile[0].start(half, block)

    owner = lane_ids(both, LANES) % (LANES // 2) // rank
    owns = [jnp.where(owner == n, 1.0, 0.0).astype(jnp.bfloat16) for n in range(per_half)]

    def spread(tiles, target, piece):
        half, block = place(piece)
        tiles.wait(half, block)
        own = pl.ds(half * per_half, per_half)

        def body(inner, freq):
            forms = []
            for tile in range(tile_size):
                arrived = tiles.recv[half, block, tile, inner].astype(jnp.float32)
                for row in range(rows):
                    part = arrived[row * virtual : (row + 1) * virtual]
                    forms.append(
                        jnp.concatenate([part * sign, swap(part)], 0).astype(jnp.bfloat16)
                    )
            matrix = jnp.concatenate(
                [jnp.concatenate([form * own_n for form in forms], 1) for own_n in owns], 0
            )
            factors = jnp.concatenate(
                [
                    right[freq, row, own, part].reshape(per_half * rank, width)
                    for row in range(row_tiles)
                    for part in range(2)
                ],
                0,
            )
            total = nn_dot(matrix, factors) * steps_ref[freq]
            for col in range(per_half):
                for lane in range(lanes_each):
                    narrow[col * lanes_each + lane, inner * both : (inner + 1) * both] = total[
                        col * both : (col + 1) * both, lane * LANES : (lane + 1) * LANES
                    ]

        each_freq(block, body)
        for peer in range(per_half * lanes_each):
            for pair in range(virtual // 2):
                target.send[half, block, peer, pair] = jnp.concatenate(
                    [
                        narrow[peer, pl.ds(2 * pair + n, tall, stride=virtual), :]
                        for n in range(2)
                    ],
                    0,
                ).astype(jnp.bfloat16)
        target.start(half, block)

    def shrink(second, source, target, half):
        for block in range(blocks):
            source.wait(half, block)
        times = tables.shape[1]
        turn = jnp.where(
            lax.broadcasted_iota(jnp.int32, (times, 2 * LANES), 0) % 2 == 0, 1.0, -1.0
        )
        lane = lane_ids(1, 2 * LANES)
        for pair in range(virtual // 2):
            arrived = [
                source.recv[half, block, peer, pair].astype(jnp.float32)
                for peer in range(source.size)
                for block in range(blocks)
            ]
            spectrum = jnp.concatenate(
                [
                    jnp.concatenate([part[n * tall : (n + 1) * tall] for part in arrived], 0)
                    for n in range(2)
                ],
                1,
            ).astype(jnp.bfloat16)
            signal = nn_dot(tables[0], spectrum) + nn_dot(tables[1], spectrum)
            if second:
                signal += kept[half, pair]
            level = jnp.where(lane < LANES, levels_ref[2 * pair], levels_ref[2 * pair + 1])
            shrunk = signal - jnp.minimum(jnp.maximum(signal, -level), level)
            if not second:
                mean = jnp.sum(shrunk * turn, 0, keepdims=True) * (1.0 / times)
                kept[half, pair] = shrunk - turn * mean
            high, low = split_two(shrunk)
            back = nn_dot(tables[2], high) + nn_dot(tables[3], high) + nn_dot(tables[2], low)
            for peer in range(target.size):
                for block in range(blocks):
                    at = (peer * blocks + block) * tall
                    target.send[half, block, peer, pair] = jnp.concatenate(
                        [back[at : at + tall, n * LANES : (n + 1) * LANES] for n in range(2)], 0
                    ).astype(jnp.bfloat16)

    def unshuffle(source, half, block, store):
        source.wait(half, block)
        for peer in range(source.size):
            for pair in range(virtual // 2):
                gathered[peer, pair * both : (pair + 1) * both] = source.recv[
                    half, block, peer, pair
                ].astype(jnp.float32)
        for freq in range(at_once):
            for peer in range(source.size):
                values = [
                    gathered[peer, pl.ds(2 * freq + part, virtual, stride=tall), :]
                    for part in range(2)
                ]
                store(freq, peer, jnp.concatenate(values, 0).astype(jnp.bfloat16))

    def store_field(freq, peer, values):
        fields[freq, :, peer * LANES : (peer + 1) * LANES] = values

    low_part = lane_ids(virtual, LANES) % (LANES // 2) < rows * rank

    def project(target, half, block):
        groups = row_tiles // per_half
        per_group = per_half // rows

        def body(inner, freq):
            coefs = []
            for col in range(per_half):
                field = fields[inner, :, col * width : (col + 1) * width]
                factors = jnp.concatenate(
                    [
                        right[
                            freq, group * per_half : (group + 1) * per_half,
                            half * per_half + col, part,
                        ].reshape(per_half * rank, width)
                        for group in range(groups)
                        for part in range(2)
                    ],
                    0,
                )
                product = nt_dot(field, factors)
                weight = weight_right[freq, pl.ds(half * per_half + col, 1), :]
                coefs.append(
                    [
                        (
                            product[:virtual, at : at + LANES] * sign
                            + swap(product[virtual:, at : at + LANES])
                        )
                        * weight[:, at : at + LANES]
                        for at in range(0, groups * LANES, LANES)
                    ]
                )
            shift = rows * rank
            for group in range(groups):
                lower, upper = [], []
                for col in range(0, per_half, per_group):
                    a, b = coefs[col][group], coefs[col + 1][group]
                    lower.append(jnp.where(low_part, a, pltpu.roll(b, shift, 1)))
                    upper.append(jnp.where(low_part, pltpu.roll(a, LANES - shift, 1), b))
                for n, packed in enumerate((lower, upper)):
                    target.send[half, block, group * per_group + n, inner] = jnp.concatenate(
                        packed, 0
                    ).astype(jnp.bfloat16)

        each_freq(block, body)
        target.start(half, block)

    row_owner = lane_ids(both, LANES) % (rows * rank) // rank
    row_owns = [jnp.where(row_owner == n, 1.0, 0.0).astype(jnp.bfloat16) for n in range(rows)]

    def image(source, half, block, inner, freq):
        per_group = per_half // rows
        forms = []
        for tile in range(tile_size):
            arrived = source.recv[half, block, tile, inner].astype(jnp.float32)
            for n in range(rows):
                part = arrived[n * virtual : (n + 1) * virtual]
                forms.append(jnp.concatenate([part * sign, swap(part)], 0).astype(jnp.bfloat16))
        matrix = jnp.concatenate(
            [jnp.concatenate([form * own for form in forms], 1) for own in row_owns], 0
        )
        factors = jnp.concatenate(
            [
                left[freq, row, tile, half * per_half + n * per_group + col, part]
                for tile in range(tile_size)
                for n in range(rows)
                for part in range(2)
                for col in range(per_group)
                for row in range(rows)
            ],
            0,
        )
        return nn_dot(matrix, factors)

    def first_image(block):
        over_tile[1].wait(0, block)

        def body(inner, freq):
            part = image(over_tile[1], 0, block, inner, freq)
            for row in range(rows):
                residual[freq, row] = (
                    recorded[freq, :, :, row * width : (row + 1) * width].reshape(both, width)
                    - part[row * both : (row + 1) * both]
                )

        each_freq(block, body)

    def last_image(block):
        over_tile[1].wait(1, block)

        def body(inner, freq):
            part = image(over_tile[1], 1, block, inner, freq)
            for row in range(rows):
                residual[freq, row] = residual[freq, row] - part[row * both : (row + 1) * both]

        each_freq(block, body)

    def last_dual(half, block):
        def body(inner, freq):
            dual(
                over_tile[2], half, block, inner, freq,
                lambda row: residual[freq, row].astype(jnp.bfloat16),
            )

        each_freq(block, body)
        over_tile[2].start(half, block)

    for copy in small[:2]:
        copy.start()
    for piece in range(AHEAD):
        fetch_left(piece).start()
        if piece == 0:
            small[2].start()

    barrier = pltpu.get_barrier_semaphore()
    count = 0
    for exchange in (over_tile[0], over_freq[0]):
        for peer in exchange.peers():
            pl.semaphore_signal(
                barrier, inc=1, device_id={exchange.axis: peer},
                device_id_type=pl.DeviceIdType.MESH,
            )
            count += 1

    for copy in small[:2]:
        copy.wait()
    tiles = ranks_ref.shape[2]
    lines = freqs * row_tiles
    parts = stacked_parts(
        ranks_ref[...].reshape(lines, tiles),
        (scales_ref[:, 0] * scales_ref[:, 1]).reshape(lines, tiles),
    )
    stacked = jnp.concatenate(parts, 0)
    for half in range(halves):
        lane = lane_ids(tiles, share)
        owner_tile = (
            lane // LANES * (halves * per_half) + half * per_half + lane % (LANES // 2) // rank
        )
        pick = jnp.where(
            owner_tile == lax.broadcasted_iota(jnp.int32, (tiles, share), 0), 1.0, 0.0
        ).astype(jnp.bfloat16)
        weight_left[half] = weights_of(nn_dot(stacked, pick), lines, rank)

    small[2].wait()

    @pl.loop(0, pieces + TILE_LAG)
    def _(step):
        @pl.when(step + AHEAD < pieces)
        def _():
            fetch_left(step + AHEAD).start()

        @pl.when(step < pieces)
        def _():
            fetch_right(step).start()
            fetch_left(step).wait()
            first_dual(step)

        @pl.when(step == pieces - 1)
        def _():
            small[3].start()
            cols = weight_right.shape[1]
            mine = lax.axis_index("tile") * cols
            select = jnp.where(
                lane_ids(cols, tiles) == mine + lax.broadcasted_iota(jnp.int32, (cols, tiles), 0),
                1.0, 0.0,
            ).astype(jnp.bfloat16)
            turned = jnp.concatenate([nt_dot(select, part) for part in parts], 0).astype(
                jnp.bfloat16
            )
            lanes = weight_right.shape[2]
            lane = lane_ids(lines, lanes)
            owner_row = lane // LANES * per_half + lane % (LANES // 2) // rank

            @pl.loop(0, freqs)
            def _(freq):
                pick = jnp.where(
                    lax.broadcasted_iota(jnp.int32, (lines, lanes), 0)
                    == owner_row + freq * row_tiles,
                    1.0, 0.0,
                ).astype(jnp.bfloat16)
                weight_right[freq] = weights_of(nn_dot(turned, pick), cols, rank)

            small[3].wait()

        @pl.when(step >= TILE_LAG)
        def _():
            piece = step - TILE_LAG
            fetch_right(piece).wait()
            spread(over_tile[0], over_freq[0], piece)

    @pl.loop(0, halves)
    def _(half):
        shrink(False, over_freq[0], over_freq[1], half)

        @pl.loop(0, blocks)
        def _(block):
            @pl.when(half * blocks + block < WINDOW)
            def _():
                over_freq[1].start(half, block)

    @pl.loop(0, pieces)
    def _(step):
        half, block = place(step)
        unshuffle(over_freq[1], half, block, store_field)

        @pl.when(step + WINDOW < pieces)
        def _():
            over_freq[1].start(*place(step + WINDOW))

        project(over_tile[1], half, block)

        @pl.when(half == halves - 1)
        def _():
            first_image(block)

    @pl.loop(0, pieces + SECOND_LAG)
    def _(step):
        half, block = place(step)

        @pl.when(half == 0)
        def _():
            last_image(block)

        @pl.when(step < pieces)
        def _():
            last_dual(half, block)

        @pl.when(step >= SECOND_LAG)
        def _():
            spread(over_tile[2], over_freq[2], step - SECOND_LAG)

    @pl.loop(0, halves)
    def _(half):
        shrink(True, over_freq[2], over_freq[3], half)

        @pl.loop(0, blocks)
        def _(block):
            over_freq[3].start(half, block)

    half_width = per_half * width

    def put(half, block):
        part = (
            pl.ds(block * at_once, at_once), slice(None), pl.ds(half * half_width, half_width)
        )
        return pltpu.make_async_copy(out_ref.at[half, block], out_hbm.at[part], out_sem.at[half, block])

    @pl.loop(0, pieces)
    def _(step):
        half, block = place(step)

        def store(freq, peer, values):
            out_ref[half, block, freq, :, peer * LANES : (peer + 1) * LANES] = values

        unshuffle(over_freq[3], half, block, store)
        put(half, block).start()

    for half in range(halves):
        for block in range(blocks):
            put(half, block).wait()
    for exchange in over_tile + over_freq:
        exchange.finish()


AHEAD = 3
TILE_LAG = 4
SECOND_LAG = 3
WINDOW = 3


def table_parts():
    times = 2 * F
    freq = np.arange(F)[:, None]
    angles = (freq * np.arange(times)[None, :] % times) * (2.0 * math.pi / times)
    scaling = np.where(freq == 0, math.sqrt(1.0 / times), math.sqrt(2.0 / times))
    table = np.stack([scaling * np.cos(angles), -scaling * np.sin(angles)], 1)
    table = table.reshape(2 * F, times).astype(np.float32)
    high = table.astype(jnp.bfloat16)
    low = (table - high.astype(np.float32)).astype(jnp.bfloat16)
    return jnp.asarray(np.stack([high.T, low.T, high, low]))


def vmem():
    return pl.BlockSpec(memory_space=pltpu.VMEM)


def smem():
    return pl.BlockSpec(memory_space=pltpu.SMEM)


def per_device(
    left_factor, right_factor, tile_ranks, tile_scales, recorded, step_sizes, thresholds
):
    freqs, rows_here, col_tiles, _, rank, width = left_factor.shape
    row_tiles, cols_here = right_factor.shape[1:3]
    virtual = recorded.shape[2]
    tile_size = col_tiles // cols_here
    freq_size = lax.axis_size("freq")
    per_half = LANES // (2 * rank)
    halves = cols_here // per_half
    at_once = 4
    blocks = freqs // at_once
    both = 2 * virtual
    left_factor = left_factor.reshape(freqs, rows_here, tile_size, cols_here, 2, rank, width)
    out_shape = (freqs, both, cols_here * width)
    dma = pltpu.SemaphoreType.DMA
    tables = table_parts()
    bf16, f32 = jnp.bfloat16, jnp.float32
    tile_buffer = pltpu.VMEM(
        (3, halves, blocks, tile_size, at_once, rows_here * virtual, LANES), bf16
    )
    freq_buffer = pltpu.VMEM(
        (4, halves, blocks, freq_size, virtual // 2, 2 * 2 * at_once, LANES), bf16
    )
    estimate = pl.pallas_call(
        whole_kernel,
        out_shape=jax.ShapeDtypeStruct(out_shape, bf16),
        in_specs=[smem(), smem()] + [pl.BlockSpec(memory_space=pl.ANY)] * 6,
        out_specs=pl.BlockSpec(memory_space=pl.ANY),
        scratch_shapes=[
            pltpu.VMEM(tables.shape, bf16),
            pltpu.VMEM(left_factor.shape, bf16),
            pltpu.VMEM(right_factor.shape, bf16),
            pltpu.VMEM(recorded.shape, f32),
            pltpu.VMEM(tile_ranks.shape, jnp.int32),
            pltpu.VMEM(tile_scales.shape, f32),
            pltpu.VMEM((halves, blocks, at_once, both, per_half * width), bf16),
            dma((halves, blocks)),
            dma((halves, blocks)),
            dma((4,)),
            dma((halves, blocks)),
            pltpu.VMEM((halves, freqs * row_tiles, tile_size * LANES), f32),
            pltpu.VMEM((freqs, cols_here, row_tiles * 2 * rank), f32),
            pltpu.VMEM((freqs, rows_here, both, width), f32),
            pltpu.VMEM((freq_size, at_once * both, LANES), f32),
            pltpu.VMEM((freq_size, at_once * both, LANES), f32),
            pltpu.VMEM((at_once, both, per_half * width), bf16),
            pltpu.VMEM((halves, virtual // 2, 2 * F, 2 * LANES), f32),
            tile_buffer,
            tile_buffer,
            freq_buffer,
            freq_buffer,
            dma((3,)),
            dma((3, halves, blocks)),
            dma((4,)),
            dma((4, halves, blocks)),
        ],
        compiler_params=pltpu.CompilerParams(
            vmem_limit_bytes=58 << 20,
            collective_id=0,
            has_side_effects=True,
        ),
    )(
        thresholds, step_sizes, tables, left_factor, right_factor, recorded, tile_ranks,
        tile_scales,
    )
    return estimate.astype(jnp.float32).reshape(freqs, 2, virtual, cols_here * width)


def either(*arrays):
    left_factor, right_factor = arrays[:2]
    freqs, rows_here, col_tiles = left_factor.shape[:3]
    row_tiles, cols_here = right_factor.shape[1:3]
    rank, width = left_factor.shape[4:]
    freq_size = lax.axis_size("freq")
    aligned = (
        rank == 16
        and rows_here == 2
        and width % LANES == 0
        and cols_here == 2 * (LANES // (2 * rank))
        and freq_size == LANES // (2 * rank) * (width // LANES)
        and row_tiles % (LANES // (2 * rank)) == 0
        and row_tiles == rows_here * lax.axis_size("tile")
        and col_tiles == cols_here * lax.axis_size("tile")
        and arrays[4].shape[2] == 8
        and freqs % 8 == 0
        and freqs * freq_size == F
    )
    return (per_device if aligned else per_device_plain)(*arrays)


def solution(mesh):
    return jax.shard_map(
        either,
        mesh=mesh,
        in_specs=(
            P("freq", "tile", None, None, None, None),
            P("freq", None, "tile", None, None, None),
            P("freq", None, None),
            P("freq", None, None, None),
            P("freq", None, None, "tile"),
            P("freq"),
            P(),
        ),
        out_specs=P("freq", None, None, "tile"),
        check_vma=False,
    )
```

```python
import functools
import math

import jax
import jax.numpy as jnp
import numpy as np
from jax import lax
from jax.experimental import pallas as pl
from jax.experimental.pallas import tpu as pltpu
from jax.sharding import PartitionSpec as P

F = 128


def dft_tables(freq_index, time_count):
    times_row = jnp.arange(time_count, dtype=jnp.int32)
    phase_steps = (freq_index[:, None] * times_row[None, :] % time_count).astype(jnp.float32)
    angles = phase_steps * (2.0 * math.pi / time_count)
    scaling = jnp.where(
        freq_index == 0, math.sqrt(1.0 / time_count), math.sqrt(2.0 / time_count)
    ).astype(jnp.float32)
    return (scaling[:, None] * jnp.cos(angles), scaling[:, None] * jnp.sin(angles))


def slot_weights(tile_ranks, tile_scales, rank_max):
    slot_index = jnp.arange(rank_max, dtype=jnp.int32)
    live_slots = (slot_index < tile_ranks[..., None]).astype(jnp.float32)
    return (tile_scales[:, 0] * tile_scales[:, 1])[..., None] * live_slots


def per_device_plain(
    left_factor, right_factor, tile_ranks, tile_scales, recorded, step_sizes, thresholds
):
    freqs_here = left_factor.shape[0]
    rows_here = left_factor.shape[1]
    col_tiles = left_factor.shape[2]
    rank_max = left_factor.shape[4]
    tile_width = left_factor.shape[5]
    row_tiles = right_factor.shape[1]
    cols_here = right_factor.shape[2]
    virtual = recorded.shape[2]
    tile_pos = lax.axis_index("tile")
    columns_here = cols_here * tile_width
    time_count = 2 * F
    highest = lax.Precision.HIGHEST
    weights = slot_weights(tile_ranks, tile_scales, rank_max)
    weights_right = lax.dynamic_slice_in_dim(weights, tile_pos * cols_here, cols_here, 2)
    weights_left = lax.dynamic_slice_in_dim(weights, tile_pos * rows_here, rows_here, 1)
    left_real = left_factor[:, :, :, 0]
    left_imag = left_factor[:, :, :, 1]
    right_real = right_factor[:, :, :, 0]
    right_imag = right_factor[:, :, :, 1]
    cos_all, sin_all = dft_tables(jnp.arange(F, dtype=jnp.int32), time_count)

    def gradient(residual):
        halves = residual.astype(jnp.bfloat16).reshape(
            freqs_here, 2, virtual, rows_here, tile_width
        )

        def contract_left(matrix, vectors):
            return jnp.einsum(
                "fijkq,fviq->fijkv", matrix, vectors, preferred_element_type=jnp.float32
            )

        dual_real = contract_left(left_real, halves[:, 0]) + contract_left(left_imag, halves[:, 1])
        dual_imag = contract_left(left_real, halves[:, 1]) - contract_left(left_imag, halves[:, 0])
        duals = (
            jnp.stack([dual_real, dual_imag], 3) * weights_left[:, :, :, None, :, None]
        ).astype(jnp.bfloat16)
        duals = duals.reshape(freqs_here, rows_here, col_tiles, 2, rank_max * virtual)
        arrived = lax.all_to_all(duals, "tile", split_axis=2, concat_axis=1, tiled=True)
        arrived = arrived.reshape(freqs_here, row_tiles, cols_here, 2, rank_max, virtual)

        def spread(matrix, vectors):
            return jnp.einsum(
                "fijkp,fijkv->fvjp", matrix, vectors, preferred_element_type=jnp.float32
            )

        grad_real = spread(right_real, arrived[:, :, :, 0]) - spread(
            right_imag, arrived[:, :, :, 1]
        )
        grad_imag = spread(right_real, arrived[:, :, :, 1]) + spread(
            right_imag, arrived[:, :, :, 0]
        )
        return jnp.stack([grad_real, grad_imag], 1).reshape(freqs_here, 2, virtual, columns_here)

    def to_time(wavefield):
        swapped = lax.all_to_all(wavefield, "freq", split_axis=3, concat_axis=0, tiled=True)
        return jnp.einsum("fvn,ft->nvt", swapped[:, 0], cos_all, precision=highest) - jnp.einsum(
            "fvn,ft->nvt", swapped[:, 1], sin_all, precision=highest
        )

    def shrink(signal):
        excess = jnp.abs(signal) - thresholds[None, :, None]
        return jnp.sign(signal) * jnp.maximum(excess, 0.0)

    def to_freq(signal):
        real_part = jnp.einsum("nvt,ft->fvn", signal, cos_all, precision=highest)
        imag_part = -jnp.einsum("nvt,ft->fvn", signal, sin_all, precision=highest)
        return lax.all_to_all(
            jnp.stack([real_part, imag_part], 1), "freq", split_axis=0, concat_axis=3, tiled=True
        )

    scaled = step_sizes[:, None, None, None]
    first = to_freq(shrink(to_time(scaled * gradient(recorded))))
    halves = first.astype(jnp.bfloat16).reshape(freqs_here, 2, virtual, cols_here, tile_width)

    def project(matrix, vectors):
        return jnp.einsum("fijkp,fvjp->fijkv", matrix, vectors, preferred_element_type=jnp.float32)

    coef_real = project(right_real, halves[:, 0]) + project(right_imag, halves[:, 1])
    coef_imag = project(right_real, halves[:, 1]) - project(right_imag, halves[:, 0])
    coeffs = (jnp.stack([coef_real, coef_imag], 3) * weights_right[:, :, :, None, :, None]).astype(
        jnp.bfloat16
    )
    coeffs = coeffs.reshape(freqs_here, row_tiles, cols_here, 2, rank_max * virtual)
    arrived = lax.all_to_all(coeffs, "tile", split_axis=1, concat_axis=2, tiled=True)
    arrived = arrived.reshape(freqs_here, rows_here, col_tiles, 2, rank_max, virtual)

    def expand(matrix, vectors):
        return jnp.einsum("fijkq,fijkv->fviq", matrix, vectors, preferred_element_type=jnp.float32)

    image_real = expand(left_real, arrived[:, :, :, 0]) - expand(left_imag, arrived[:, :, :, 1])
    image_imag = expand(left_real, arrived[:, :, :, 1]) + expand(left_imag, arrived[:, :, :, 0])
    return to_freq(
        shrink(
            to_time(
                first
                + scaled
                * gradient(
                    recorded
                    - jnp.stack([image_real, image_imag], 1).reshape(
                        freqs_here, 2, virtual, rows_here * tile_width
                    )
                )
            )
        )
    )


LANES = 128


def lane_ids(rows, lanes):
    return lax.broadcasted_iota(jnp.int32, (rows, lanes), 1)


def nt_dot(a, b):
    return lax.dot_general(a, b, (((1,), (1,)), ((), ())), preferred_element_type=jnp.float32)


def nn_dot(a, b):
    return jnp.dot(a, b, preferred_element_type=jnp.float32)


def swap(values):
    return pltpu.roll(values, LANES // 2, 1)


def part_sign(rows):
    return jnp.where(lane_ids(rows, LANES) < LANES // 2, 1.0, -1.0)


def stacked_parts(ranks, scales):
    high = scales.astype(jnp.bfloat16)
    rest = scales - high.astype(jnp.float32)
    middle = rest.astype(jnp.bfloat16)
    low = (rest - middle.astype(jnp.float32)).astype(jnp.bfloat16)
    return high, middle, low, ranks.astype(jnp.float32).astype(jnp.bfloat16)


def weights_of(product, rows, rank):
    high, middle, low, ranks = [product[n * rows : (n + 1) * rows] for n in range(4)]
    slot = (lane_ids(rows, product.shape[1]) % rank).astype(jnp.float32)
    return jnp.where(slot < ranks - 0.5, high + middle + low, 0.0)


class Exchange:
    def __init__(self, axis, send, recv, send_sem, recv_sem):
        self.axis, self.send, self.recv = axis, send, recv
        self.send_sem, self.recv_sem = send_sem, recv_sem
        self.size = send.shape[2]
        self.me = lax.axis_index(axis)

    def peers(self):
        return [lax.rem(self.me + step, self.size) for step in range(1, self.size)]

    def start(self, half, block):
        for peer in self.peers():
            pltpu.make_async_remote_copy(
                src_ref=self.send.at[half, block, peer],
                dst_ref=self.recv.at[half, block, self.me],
                send_sem=self.send_sem,
                recv_sem=self.recv_sem.at[half, block],
                device_id={self.axis: peer},
                device_id_type=pl.DeviceIdType.MESH,
            ).start()
        self.recv[half, block, self.me] = self.send[half, block, self.me]

    def wait(self, half, block):
        others = pl.ds(0, self.size - 1)
        pltpu.make_async_remote_copy(
            src_ref=self.send.at[half, block, others],
            dst_ref=self.recv.at[half, block, others],
            send_sem=self.send_sem,
            recv_sem=self.recv_sem.at[half, block],
            device_id={self.axis: self.peers()[0]},
            device_id_type=pl.DeviceIdType.MESH,
        ).wait_recv()

    def finish(self):
        others = pl.ds(0, self.size - 1)
        pltpu.make_async_remote_copy(
            src_ref=self.send.at[:, :, others],
            dst_ref=self.recv.at[:, :, others],
            send_sem=self.send_sem,
            recv_sem=self.recv_sem.at[0, 0],
            device_id={self.axis: self.peers()[0]},
            device_id_type=pl.DeviceIdType.MESH,
        ).wait_send()


def whole_kernel(
    levels_ref, steps_ref, tables_hbm, left_hbm, right_hbm, recorded_hbm, ranks_hbm, scales_hbm,
    out_hbm,
    tables, left, right, recorded, ranks_ref, scales_ref, out_ref,
    left_sem, right_sem, small_sem, out_sem,
    weight_left, weight_right, residual, narrow, gathered, fields, kept,
    tile_send, tile_recv, freq_send, freq_recv, tile_ssem, tile_rsem, freq_ssem, freq_rsem,
):
    freqs, rows, tile_size, _, _, rank, width = left.shape
    row_tiles = right.shape[1]
    virtual = recorded.shape[2]
    per_half = LANES // (2 * rank)
    lanes_each = width // LANES
    halves, blocks = tile_send.shape[1:3]
    at_once = tile_send.shape[4]
    tall = 2 * at_once
    both = 2 * virtual
    pieces = halves * blocks
    share = tile_size * LANES
    first_row = lax.axis_index("tile") * rows
    sign = part_sign(virtual)
    over_tile = [
        Exchange("tile", tile_send.at[n], tile_recv.at[n], tile_ssem.at[n], tile_rsem.at[n])
        for n in range(tile_send.shape[0])
    ]
    over_freq = [
        Exchange("freq", freq_send.at[n], freq_recv.at[n], freq_ssem.at[n], freq_rsem.at[n])
        for n in range(freq_send.shape[0])
    ]
    small = [
        pltpu.make_async_copy(source, target, small_sem.at[n])
        for n, (source, target) in enumerate(
            [(ranks_hbm, ranks_ref), (scales_hbm, scales_ref), (recorded_hbm, recorded),
             (tables_hbm, tables)]
        )
    ]

    def place(piece):
        return piece // blocks, piece % blocks

    def fetch_left(piece):
        half, block = place(piece)
        part = (pl.ds(block * at_once, at_once), slice(None), slice(None), pl.ds(half * per_half, per_half))
        return pltpu.make_async_copy(left_hbm.at[part], left.at[part], left_sem.at[half, block])

    def fetch_right(piece):
        half, block = place(piece)
        part = (pl.ds(block * at_once, at_once), slice(None), pl.ds(half * per_half, per_half))
        return pltpu.make_async_copy(right_hbm.at[part], right.at[part], right_sem.at[half, block])

    def each_freq(block, body):
        for inner in range(at_once):
            body(inner, block * at_once + inner)

    def left_rows(freq, row, half):
        own = pl.ds(half * per_half, per_half)
        return jnp.concatenate(
            [
                left[freq, row, tile, own, part].reshape(per_half * rank, width)
                for tile in range(tile_size)
                for part in range(2)
            ],
            0,
        )

    def dual(exchange, half, block, inner, freq, field_of):
        duals = []
        for row in range(rows):
            product = nt_dot(field_of(row), left_rows(freq, row, half))
            weight = weight_left[half, pl.ds(freq * row_tiles + first_row + row, 1), :]
            duals.append(
                [
                    (
                        product[:virtual, at : at + LANES] * sign
                        + swap(product[virtual:, at : at + LANES])
                    )
                    * weight[:, at : at + LANES]
                    for at in range(0, share, LANES)
                ]
            )
        for tile in range(tile_size):
            exchange.send[half, block, tile, inner] = jnp.concatenate(
                [duals[row][tile] for row in range(rows)], 0
            ).astype(jnp.bfloat16)

    def first_dual(piece):
        half, block = place(piece)

        def body(inner, freq):
            dual(
                over_tile[0], half, block, inner, freq,
                lambda row: recorded[freq, :, :, row * width : (row + 1) * width]
                .reshape(both, width)
                .astype(jnp.bfloat16),
            )

        each_freq(block, body)

        @pl.when(piece == 0)
        def _():
            pl.semaphore_wait(barrier, count)

        over_tile[0].start(half, block)

    owner = lane_ids(both, LANES) % (LANES // 2) // rank
    owns = [jnp.where(owner == n, 1.0, 0.0).astype(jnp.bfloat16) for n in range(per_half)]

    def spread(tiles, target, piece):
        half, block = place(piece)
        tiles.wait(half, block)
        own = pl.ds(half * per_half, per_half)

        def body(inner, freq):
            forms = []
            for tile in range(tile_size):
                arrived = tiles.recv[half, block, tile, inner].astype(jnp.float32)
                for row in range(rows):
                    part = arrived[row * virtual : (row + 1) * virtual]
                    forms.append(
                        jnp.concatenate([part * sign, swap(part)], 0).astype(jnp.bfloat16)
                    )
            matrix = jnp.concatenate(
                [jnp.concatenate([form * own_n for form in forms], 1) for own_n in owns], 0
            )
            factors = jnp.concatenate(
                [
                    right[freq, row, own, part].reshape(per_half * rank, width)
                    for row in range(row_tiles)
                    for part in range(2)
                ],
                0,
            )
            total = nn_dot(matrix, factors) * steps_ref[freq]
            for col in range(per_half):
                for lane in range(lanes_each):
                    narrow[col * lanes_each + lane, inner * both : (inner + 1) * both] = total[
                        col * both : (col + 1) * both, lane * LANES : (lane + 1) * LANES
                    ]

        each_freq(block, body)
        for peer in range(per_half * lanes_each):
            for pair in range(virtual // 2):
                target.send[half, block, peer, pair] = jnp.concatenate(
                    [
                        narrow[peer, pl.ds(2 * pair + n, tall, stride=virtual), :]
                        for n in range(2)
                    ],
                    0,
                ).astype(jnp.bfloat16)
        target.start(half, block)

    def shrink(second, source, target, half):
        for block in range(blocks):
            source.wait(half, block)
        times = tables.shape[1]
        turn = jnp.where(
            lax.broadcasted_iota(jnp.int32, (times, 2 * LANES), 0) % 2 == 0, 1.0, -1.0
        )
        lane = lane_ids(1, 2 * LANES)
        for pair in range(virtual // 2):
            arrived = [
                source.recv[half, block, peer, pair].astype(jnp.float32)
                for peer in range(source.size)
                for block in range(blocks)
            ]
            spectrum = jnp.concatenate(
                [
                    jnp.concatenate([part[n * tall : (n + 1) * tall] for part in arrived], 0)
                    for n in range(2)
                ],
                1,
            ).astype(jnp.bfloat16)
            signal = nn_dot(tables[0], spectrum) + nn_dot(tables[1], spectrum)
            if second:
                signal += kept[half, pair]
            level = jnp.where(lane < LANES, levels_ref[2 * pair], levels_ref[2 * pair + 1])
            shrunk = signal - jnp.minimum(jnp.maximum(signal, -level), level)
            if not second:
                mean = jnp.sum(shrunk * turn, 0, keepdims=True) * (1.0 / times)
                kept[half, pair] = shrunk - turn * mean
            rounded = shrunk.astype(jnp.bfloat16)
            back = nn_dot(tables[2], rounded) + nn_dot(tables[3], rounded)
            for peer in range(target.size):
                for block in range(blocks):
                    at = (peer * blocks + block) * tall
                    target.send[half, block, peer, pair] = jnp.concatenate(
                        [back[at : at + tall, n * LANES : (n + 1) * LANES] for n in range(2)], 0
                    ).astype(jnp.bfloat16)

    def unshuffle(source, half, block, store):
        source.wait(half, block)
        for peer in range(source.size):
            for pair in range(virtual // 2):
                gathered[peer, pair * both : (pair + 1) * both] = source.recv[
                    half, block, peer, pair
                ].astype(jnp.float32)
        for freq in range(at_once):
            for peer in range(source.size):
                values = [
                    gathered[peer, pl.ds(2 * freq + part, virtual, stride=tall), :]
                    for part in range(2)
                ]
                store(freq, peer, jnp.concatenate(values, 0).astype(jnp.bfloat16))

    def store_field(freq, peer, values):
        fields[freq, :, peer * LANES : (peer + 1) * LANES] = values

    low_part = lane_ids(virtual, LANES) % (LANES // 2) < rows * rank

    def project(target, half, block):
        groups = row_tiles // per_half
        per_group = per_half // rows

        def body(inner, freq):
            coefs = []
            for col in range(per_half):
                field = fields[inner, :, col * width : (col + 1) * width]
                factors = jnp.concatenate(
                    [
                        right[
                            freq, group * per_half : (group + 1) * per_half,
                            half * per_half + col, part,
                        ].reshape(per_half * rank, width)
                        for group in range(groups)
                        for part in range(2)
                    ],
                    0,
                )
                product = nt_dot(field, factors)
                weight = weight_right[freq, pl.ds(half * per_half + col, 1), :]
                coefs.append(
                    [
                        (
                            product[:virtual, at : at + LANES] * sign
                            + swap(product[virtual:, at : at + LANES])
                        )
                        * weight[:, at : at + LANES]
                        for at in range(0, groups * LANES, LANES)
                    ]
                )
            shift = rows * rank
            for group in range(groups):
                lower, upper = [], []
                for col in range(0, per_half, per_group):
                    a, b = coefs[col][group], coefs[col + 1][group]
                    lower.append(jnp.where(low_part, a, pltpu.roll(b, shift, 1)))
                    upper.append(jnp.where(low_part, pltpu.roll(a, LANES - shift, 1), b))
                for n, packed in enumerate((lower, upper)):
                    target.send[half, block, group * per_group + n, inner] = jnp.concatenate(
                        packed, 0
                    ).astype(jnp.bfloat16)

        each_freq(block, body)
        target.start(half, block)

    row_owner = lane_ids(both, LANES) % (rows * rank) // rank
    row_owns = [jnp.where(row_owner == n, 1.0, 0.0).astype(jnp.bfloat16) for n in range(rows)]

    def image(source, half, block, inner, freq):
        per_group = per_half // rows
        forms = []
        for tile in range(tile_size):
            arrived = source.recv[half, block, tile, inner].astype(jnp.float32)
            for n in range(rows):
                part = arrived[n * virtual : (n + 1) * virtual]
                forms.append(jnp.concatenate([part * sign, swap(part)], 0).astype(jnp.bfloat16))
        matrix = jnp.concatenate(
            [jnp.concatenate([form * own for form in forms], 1) for own in row_owns], 0
        )
        factors = jnp.concatenate(
            [
                left[freq, row, tile, half * per_half + n * per_group + col, part]
                for tile in range(tile_size)
                for n in range(rows)
                for part in range(2)
                for col in range(per_group)
                for row in range(rows)
            ],
            0,
        )
        return nn_dot(matrix, factors)

    def first_image(block):
        over_tile[1].wait(0, block)

        def body(inner, freq):
            part = image(over_tile[1], 0, block, inner, freq)
            for row in range(rows):
                residual[freq, row] = (
                    recorded[freq, :, :, row * width : (row + 1) * width].reshape(both, width)
                    - part[row * both : (row + 1) * both]
                )

        each_freq(block, body)

    def last_image(block):
        over_tile[1].wait(1, block)

        def body(inner, freq):
            part = image(over_tile[1], 1, block, inner, freq)
            for row in range(rows):
                residual[freq, row] = residual[freq, row] - part[row * both : (row + 1) * both]

        each_freq(block, body)

    def last_dual(half, block):
        def body(inner, freq):
            dual(
                over_tile[2], half, block, inner, freq,
                lambda row: residual[freq, row].astype(jnp.bfloat16),
            )

        each_freq(block, body)
        over_tile[2].start(half, block)

    for copy in small[:2]:
        copy.start()
    for piece in range(AHEAD):
        fetch_left(piece).start()
        if piece == 0:
            small[2].start()

    barrier = pltpu.get_barrier_semaphore()
    count = 0
    for exchange in (over_tile[0], over_freq[0]):
        for peer in exchange.peers():
            pl.semaphore_signal(
                barrier, inc=1, device_id={exchange.axis: peer},
                device_id_type=pl.DeviceIdType.MESH,
            )
            count += 1

    for copy in small[:2]:
        copy.wait()
    tiles = ranks_ref.shape[2]
    lines = freqs * row_tiles
    parts = stacked_parts(
        ranks_ref[...].reshape(lines, tiles),
        (scales_ref[:, 0] * scales_ref[:, 1]).reshape(lines, tiles),
    )
    stacked = jnp.concatenate(parts, 0)
    for half in range(halves):
        lane = lane_ids(tiles, share)
        owner_tile = (
            lane // LANES * (halves * per_half) + half * per_half + lane % (LANES // 2) // rank
        )
        pick = jnp.where(
            owner_tile == lax.broadcasted_iota(jnp.int32, (tiles, share), 0), 1.0, 0.0
        ).astype(jnp.bfloat16)
        weight_left[half] = weights_of(nn_dot(stacked, pick), lines, rank)

    small[2].wait()

    @pl.loop(0, pieces + TILE_LAG)
    def _(step):
        @pl.when(step + AHEAD < pieces)
        def _():
            fetch_left(step + AHEAD).start()

        @pl.when(step < pieces)
        def _():
            fetch_right(step).start()
            fetch_left(step).wait()
            first_dual(step)

        @pl.when(step == pieces - 1)
        def _():
            small[3].start()
            cols = weight_right.shape[1]
            mine = lax.axis_index("tile") * cols
            select = jnp.where(
                lane_ids(cols, tiles) == mine + lax.broadcasted_iota(jnp.int32, (cols, tiles), 0),
                1.0, 0.0,
            ).astype(jnp.bfloat16)
            turned = jnp.concatenate([nt_dot(select, part) for part in parts], 0).astype(
                jnp.bfloat16
            )
            lanes = weight_right.shape[2]
            lane = lane_ids(lines, lanes)
            owner_row = lane // LANES * per_half + lane % (LANES // 2) // rank

            @pl.loop(0, freqs)
            def _(freq):
                pick = jnp.where(
                    lax.broadcasted_iota(jnp.int32, (lines, lanes), 0)
                    == owner_row + freq * row_tiles,
                    1.0, 0.0,
                ).astype(jnp.bfloat16)
                weight_right[freq] = weights_of(nn_dot(turned, pick), cols, rank)

            small[3].wait()

        @pl.when(step >= TILE_LAG)
        def _():
            piece = step - TILE_LAG
            fetch_right(piece).wait()
            spread(over_tile[0], over_freq[0], piece)

    @pl.loop(0, halves)
    def _(half):
        shrink(False, over_freq[0], over_freq[1], half)

        @pl.loop(0, blocks)
        def _(block):
            @pl.when(half * blocks + block < WINDOW)
            def _():
                over_freq[1].start(half, block)

    @pl.loop(0, pieces)
    def _(step):
        half, block = place(step)
        unshuffle(over_freq[1], half, block, store_field)

        @pl.when(step + WINDOW < pieces)
        def _():
            over_freq[1].start(*place(step + WINDOW))

        project(over_tile[1], half, block)

        @pl.when(half == halves - 1)
        def _():
            first_image(block)

    @pl.loop(0, pieces + SECOND_LAG)
    def _(step):
        half, block = place(step)

        @pl.when(half == 0)
        def _():
            last_image(block)

        @pl.when(step < pieces)
        def _():
            last_dual(half, block)

        @pl.when(step >= SECOND_LAG)
        def _():
            spread(over_tile[2], over_freq[2], step - SECOND_LAG)

    @pl.loop(0, halves)
    def _(half):
        shrink(True, over_freq[2], over_freq[3], half)

        @pl.loop(0, blocks)
        def _(block):
            over_freq[3].start(half, block)

    half_width = per_half * width

    def put(half, block):
        part = (
            pl.ds(block * at_once, at_once), slice(None), pl.ds(half * half_width, half_width)
        )
        return pltpu.make_async_copy(out_ref.at[half, block], out_hbm.at[part], out_sem.at[half, block])

    @pl.loop(0, pieces)
    def _(step):
        half, block = place(step)

        def store(freq, peer, values):
            out_ref[half, block, freq, :, peer * LANES : (peer + 1) * LANES] = values

        unshuffle(over_freq[3], half, block, store)
        put(half, block).start()

    for half in range(halves):
        for block in range(blocks):
            put(half, block).wait()
    for exchange in over_tile + over_freq:
        exchange.finish()


AHEAD = 3
TILE_LAG = 4
SECOND_LAG = 3
WINDOW = 3


def table_parts():
    times = 2 * F
    freq = np.arange(F)[:, None]
    angles = (freq * np.arange(times)[None, :] % times) * (2.0 * math.pi / times)
    scaling = np.where(freq == 0, math.sqrt(1.0 / times), math.sqrt(2.0 / times))
    table = np.stack([scaling * np.cos(angles), -scaling * np.sin(angles)], 1)
    table = table.reshape(2 * F, times).astype(np.float32)
    high = table.astype(jnp.bfloat16)
    low = (table - high.astype(np.float32)).astype(jnp.bfloat16)
    return jnp.asarray(np.stack([high.T, low.T, high, low]))


def vmem():
    return pl.BlockSpec(memory_space=pltpu.VMEM)


def smem():
    return pl.BlockSpec(memory_space=pltpu.SMEM)


def per_device(
    left_factor, right_factor, tile_ranks, tile_scales, recorded, step_sizes, thresholds
):
    freqs, rows_here, col_tiles, _, rank, width = left_factor.shape
    row_tiles, cols_here = right_factor.shape[1:3]
    virtual = recorded.shape[2]
    tile_size = col_tiles // cols_here
    freq_size = lax.axis_size("freq")
    per_half = LANES // (2 * rank)
    halves = cols_here // per_half
    at_once = 4
    blocks = freqs // at_once
    both = 2 * virtual
    left_factor = left_factor.reshape(freqs, rows_here, tile_size, cols_here, 2, rank, width)
    out_shape = (freqs, both, cols_here * width)
    dma = pltpu.SemaphoreType.DMA
    tables = table_parts()
    bf16, f32 = jnp.bfloat16, jnp.float32
    tile_buffer = pltpu.VMEM(
        (3, halves, blocks, tile_size, at_once, rows_here * virtual, LANES), bf16
    )
    freq_buffer = pltpu.VMEM(
        (4, halves, blocks, freq_size, virtual // 2, 2 * 2 * at_once, LANES), bf16
    )
    estimate = pl.pallas_call(
        whole_kernel,
        out_shape=jax.ShapeDtypeStruct(out_shape, bf16),
        in_specs=[smem(), smem()] + [pl.BlockSpec(memory_space=pl.ANY)] * 6,
        out_specs=pl.BlockSpec(memory_space=pl.ANY),
        scratch_shapes=[
            pltpu.VMEM(tables.shape, bf16),
            pltpu.VMEM(left_factor.shape, bf16),
            pltpu.VMEM(right_factor.shape, bf16),
            pltpu.VMEM(recorded.shape, f32),
            pltpu.VMEM(tile_ranks.shape, jnp.int32),
            pltpu.VMEM(tile_scales.shape, f32),
            pltpu.VMEM((halves, blocks, at_once, both, per_half * width), bf16),
            dma((halves, blocks)),
            dma((halves, blocks)),
            dma((4,)),
            dma((halves, blocks)),
            pltpu.VMEM((halves, freqs * row_tiles, tile_size * LANES), f32),
            pltpu.VMEM((freqs, cols_here, row_tiles * 2 * rank), f32),
            pltpu.VMEM((freqs, rows_here, both, width), f32),
            pltpu.VMEM((freq_size, at_once * both, LANES), f32),
            pltpu.VMEM((freq_size, at_once * both, LANES), f32),
            pltpu.VMEM((at_once, both, per_half * width), bf16),
            pltpu.VMEM((halves, virtual // 2, 2 * F, 2 * LANES), f32),
            tile_buffer,
            tile_buffer,
            freq_buffer,
            freq_buffer,
            dma((3,)),
            dma((3, halves, blocks)),
            dma((4,)),
            dma((4, halves, blocks)),
        ],
        compiler_params=pltpu.CompilerParams(
            vmem_limit_bytes=58 << 20,
            collective_id=0,
            has_side_effects=True,
        ),
    )(
        thresholds, step_sizes, tables, left_factor, right_factor, recorded, tile_ranks,
        tile_scales,
    )
    return estimate.astype(jnp.float32).reshape(freqs, 2, virtual, cols_here * width)


def either(*arrays):
    left_factor, right_factor = arrays[:2]
    freqs, rows_here, col_tiles = left_factor.shape[:3]
    row_tiles, cols_here = right_factor.shape[1:3]
    rank, width = left_factor.shape[4:]
    freq_size = lax.axis_size("freq")
    aligned = (
        rank == 16
        and rows_here == 2
        and width % LANES == 0
        and cols_here == 2 * (LANES // (2 * rank))
        and freq_size == LANES // (2 * rank) * (width // LANES)
        and row_tiles % (LANES // (2 * rank)) == 0
        and row_tiles == rows_here * lax.axis_size("tile")
        and col_tiles == cols_here * lax.axis_size("tile")
        and arrays[4].shape[2] == 8
        and freqs % 8 == 0
        and freqs * freq_size == F
    )
    return (per_device if aligned else per_device_plain)(*arrays)


def solution(mesh):
    return jax.shard_map(
        either,
        mesh=mesh,
        in_specs=(
            P("freq", "tile", None, None, None, None),
            P("freq", None, "tile", None, None, None),
            P("freq", None, None),
            P("freq", None, None, None),
            P("freq", None, None, "tile"),
            P("freq"),
            P(),
        ),
        out_specs=P("freq", None, None, "tile"),
        check_vma=False,
    )
```
